256 devices in a mesh: freq: 32 (over y, x, core), tile: 8 (over z).
Axes of the slice: x: 4, y: 4, z: 8, core: 2. Of those that a mesh axis runs over, the one named last changes fastest.
Arguments:
- left_factor: bfloat16 [128, 16, 32, 2, 16, 256], P('freq', 'tile'), may hold values from -1.5 to 1.5
- right_factor: bfloat16 [128, 16, 32, 2, 16, 256], P('freq', None, 'tile'), may hold values from -0.0625 to 0.0625
- tile_ranks: int32 [128, 16, 32], P('freq'), may hold values from 1 to 16
- tile_scales: float32 [128, 2, 16, 32], P('freq'), may hold values from 0.5 to 2
- recorded: float32 [128, 2, 8, 4096], P('freq', None, None, 'tile'), may hold values from -12 to 12
- step_sizes: float32 [128], P('freq'), may hold values from 0.2 to 0.6
- thresholds: float32 [8], replicated, may hold values from 0.1 to 0.5
Outputs:
- estimate: float32 [128, 2, 8, 8192], P('freq', None, None, 'tile')
The draws below stay inside these ranges and needn't reach their ends.
Inputs may be any that keep to these rules, and one draw needn't show every extreme that they name: `tile_ranks`: rank of each tile; rank slots at and above it carry no weight.
All inputs are finite; a program needn't handle non-finite values.
Results may differ from the reference program's by a relative error of at most 0.0058.
Values may be sent and summed in bfloat16 or wider, within the bound.
No kernel may reach another device: no remote copies, remote signals or barrier semaphores. Data moves between devices by JAX's collectives and lax.ppermute only.
A program may use at most 128 MiB of HBM per device.

```python
import math
import jax
import jax.numpy as jnp
from jax import lax

TS = 256
R = 16
NV = 8
F = 128
NCT = 32
NRT = 16
NR = 4096
NC = 8192


def plant(entries, key, smallest, largest):
    longest = entries.shape.index(max(entries.shape))
    spots = []
    for shift in (0, 1):
        where = [jax.random.randint(jax.random.fold_in(key, axis), (), 0, length) for axis, length in enumerate(entries.shape)]
        where[longest] = (where[longest] + shift) % entries.shape[longest]
        spots.append(tuple(where))
    return entries.at[spots[0]].set(smallest).at[spots[1]].set(largest)


def steps_of(own_key, dims, split, low, largest):
    level = 1.0
    for axis_at, blocks in split:
        draws = jax.random.uniform(jax.random.fold_in(jax.random.fold_in(own_key, 6), axis_at), (blocks,), jnp.float32, low / len(split), largest / len(split))
        level = level * jnp.repeat(jnp.exp(draws), dims[axis_at] // blocks).reshape((-1,) + (1,) * (len(dims) - 1 - axis_at))
    return level


def normal_values(key, shape, deviation, bound, cuts=(), kind=jnp.bfloat16):
    result = deviation * jax.random.normal(key, shape, jnp.float32)
    if cuts:
        result = result * steps_of(key, shape, cuts, -0.22, 0.18)
    return jnp.clip(result, -bound, bound).astype(kind)


def setup_inputs(seed: int = 0) -> dict:
    keys = jax.random.split(jax.random.key(seed), 8)
    return {
        "left_factor": normal_values(keys[0], (F, NRT, NCT, 2, R, TS), R ** -0.5, 1.5, ((0, 32), (1, 8))),
        "right_factor": normal_values(keys[1], (F, NRT, NCT, 2, R, TS), NC ** -0.5, 0.0625, ((0, 32), (2, 8))),
        "tile_ranks": plant(jax.random.randint(keys[2], (F, NRT, NCT), 1, R + 1), jax.random.fold_in(keys[2], 1), 1, R).astype(jnp.int32),
        "tile_scales": jnp.clip(jnp.exp(math.log(2.0) - 1.3862944 * jax.random.uniform(keys[3], (F, 2, NRT, NCT), jnp.float32) ** steps_of(keys[3], (F, 2, NRT, NCT), ((0, 32),), -0.2, 0.2)), 0.5, 2.0),
        "recorded": normal_values(keys[4], (F, 2, NV, NR), 2.0, 12.0, ((0, 32), (3, 8)), jnp.float32),
        "step_sizes": jnp.clip(jnp.exp(math.log(0.6) - 1.0986123 * jax.random.uniform(keys[5], (F,), jnp.float32) ** steps_of(keys[5], (F,), ((0, 32),), -0.2, 0.2)), 0.2, 0.6),
        "thresholds": jnp.clip(jnp.exp(jax.random.uniform(keys[6], (NV,), jnp.float32, math.log(0.1), math.log(0.5))), 0.1, 0.5),
    }


def dft_tables(freq_index, time_count):
    times_row = jnp.arange(time_count, dtype=jnp.int32)
    phase_steps = (freq_index[:, None] * times_row[None, :] % time_count).astype(jnp.float32)
    angles = phase_steps * (2.0 * math.pi / time_count)
    scaling = jnp.where(freq_index == 0, math.sqrt(1.0 / time_count), math.sqrt(2.0 / time_count)).astype(jnp.float32)
    return (scaling[:, None] * jnp.cos(angles), scaling[:, None] * jnp.sin(angles))

def rounded(values):
    return lax.optimization_barrier(values.astype(jnp.bfloat16)).astype(jnp.float32)

def slot_weights(tile_ranks, tile_scales, rank_max):
    slot_index = jnp.arange(rank_max, dtype=jnp.int32)
    live_slots = (slot_index < tile_ranks[..., None]).astype(jnp.float32)
    return (tile_scales[:, 0] * tile_scales[:, 1])[..., None] * live_slots

def forward_one(left, right, weights, wavefield):
    tile_width = left.shape[-1]
    virtual = wavefield.shape[1]
    left_real = left[:, :, 0].astype(jnp.float32)
    left_imag = left[:, :, 1].astype(jnp.float32)
    right_real = right[:, :, 0].astype(jnp.float32)
    right_imag = right[:, :, 1].astype(jnp.float32)
    halves = rounded(wavefield).reshape(2, virtual, right.shape[1], tile_width)

    def project(matrix, vectors):
        return jnp.einsum('ijkp,vjp->ijkv', matrix, vectors)
    coef_real = project(right_real, halves[0]) + project(right_imag, halves[1])
    coef_imag = project(right_real, halves[1]) - project(right_imag, halves[0])
    coeffs = rounded(jnp.stack([coef_real, coef_imag], 2) * weights[:, :, None, :, None])

    def expand(matrix, vectors):
        return jnp.einsum('ijkq,ijkv->viq', matrix, vectors)
    image_real = expand(left_real, coeffs[:, :, 0]) - expand(left_imag, coeffs[:, :, 1])
    image_imag = expand(left_real, coeffs[:, :, 1]) + expand(left_imag, coeffs[:, :, 0])
    return jnp.stack([image_real, image_imag]).reshape(2, virtual, -1)

def adjoint_one(left, right, weights, residual):
    tile_width = left.shape[-1]
    virtual = residual.shape[1]
    left_real = left[:, :, 0].astype(jnp.float32)
    left_imag = left[:, :, 1].astype(jnp.float32)
    right_real = right[:, :, 0].astype(jnp.float32)
    right_imag = right[:, :, 1].astype(jnp.float32)
    halves = rounded(residual).reshape(2, virtual, left.shape[0], tile_width)

    def contract_left(matrix, vectors):
        return jnp.einsum('ijkq,viq->ijkv', matrix, vectors)
    dual_real = contract_left(left_real, halves[0]) + contract_left(left_imag, halves[1])
    dual_imag = contract_left(left_real, halves[1]) - contract_left(left_imag, halves[0])
    duals = rounded(jnp.stack([dual_real, dual_imag], 2) * weights[:, :, None, :, None])

    def spread(matrix, vectors):
        return jnp.einsum('ijkp,ijkv->vjp', matrix, vectors)
    grad_real = spread(right_real, duals[:, :, 0]) - spread(right_imag, duals[:, :, 1])
    grad_imag = spread(right_real, duals[:, :, 1]) + spread(right_imag, duals[:, :, 0])
    return jnp.stack([grad_real, grad_imag]).reshape(2, virtual, -1)

def reference(left_factor, right_factor, tile_ranks, tile_scales, recorded, step_sizes, thresholds):
    weights = slot_weights(tile_ranks, tile_scales, R)
    time_count = 2 * F
    cos_table, sin_table = dft_tables(jnp.arange(F, dtype=jnp.int32), time_count)
    highest = lax.Precision.HIGHEST

    def to_time(wavefield):
        return jnp.einsum('fvn,ft->nvt', wavefield[:, 0], cos_table, precision=highest) - jnp.einsum('fvn,ft->nvt', wavefield[:, 1], sin_table, precision=highest)

    def shrink(signal):
        excess = jnp.abs(signal) - thresholds[None, :, None]
        return jnp.sign(signal) * jnp.maximum(excess, 0.0)

    def to_freq(signal):
        real_part = jnp.einsum('nvt,ft->fvn', signal, cos_table, precision=highest)
        imag_part = -jnp.einsum('nvt,ft->fvn', signal, sin_table, precision=highest)
        return jnp.stack([real_part, imag_part], 1)

    def gradient(residual):
        return lax.map(lambda per_freq: adjoint_one(*per_freq), (left_factor, right_factor, weights, residual))

    def predict(wavefield):
        return lax.map(lambda per_freq: forward_one(*per_freq), (left_factor, right_factor, weights, wavefield))
    scaled = step_sizes[:, None, None, None]
    first = to_freq(shrink(to_time(scaled * gradient(recorded))))
    return to_freq(shrink(to_time(first + scaled * gradient(recorded - predict(first)))))
```

```python
import functools
import math

import jax
import jax.numpy as jnp
import numpy as np
from jax import lax
from jax.experimental import pallas as pl
from jax.experimental.pallas import tpu as pltpu
from jax.sharding import PartitionSpec as P

F32 = jnp.float32
BF16 = jnp.bfloat16
HIGHEST = lax.Precision.HIGHEST
NT = (((1,), (1,)), ((), ()))
INTERPRET = False


class Sizes:
    def __init__(self, left, right, recorded, tiles, groups):
        self.freqs, self.rows, self.col_tiles, _, self.slots, self.side = left.shape
        self.row_tiles, self.cols = right.shape[1], right.shape[2]
        self.virtual = recorded.shape[2]
        self.tiles, self.groups = tiles, groups
        self.lanes = self.rows * self.cols * self.slots
        self.pairs = 2 * self.freqs
        self.times = 2 * self.freqs * groups
        assert self.lanes == 128 and self.virtual == 8 and self.tiles % 2 == 0
        assert self.groups == self.virtual * self.cols and self.slots == 16


def lane_group(z, shape, which):
    lane = lax.broadcasted_iota(jnp.int32, shape, 1) % z.lanes
    if which == 0:
        return lane // (z.cols * z.slots)
    return (lane // z.slots) % z.cols


def left_block(z, u, f, c, s):
    return u[f, :, z.cols * s : z.cols * (s + 1), c].reshape(z.lanes, z.side)


def right_block(z, v, f, c, s):
    return v[f, z.rows * s : z.rows * (s + 1), :, c].reshape(z.lanes, z.side)


def block_pair(block, z, ref, f, c, pair):
    return jnp.concatenate([block(z, ref, f, c, 2 * pair), block(z, ref, f, c, 2 * pair + 1)], 0)


def finish_weights(z, scales, ranks, expand):
    wide = jnp.dot(scales, expand, precision=HIGHEST, preferred_element_type=F32)
    live = jnp.dot(ranks, expand, precision=HIGHEST, preferred_element_type=F32)
    slot = (lax.broadcasted_iota(jnp.int32, wide.shape, 1) % z.slots).astype(F32)
    return jnp.where(slot < live, wide, 0.0)


def row_weights(z, here, ranks_ref, scales_ref, f):
    rows = []
    for source in (None, ranks_ref):
        parts = []
        for r in range(z.rows):
            at = pl.ds(z.rows * here + r, 1)
            if source is None:
                one = scales_ref[f, 0, at, :] * scales_ref[f, 1, at, :]
            else:
                one = ranks_ref[f, at, :].astype(F32)
            wide = jnp.broadcast_to(one, (z.tiles, z.col_tiles))
            owner = lax.broadcasted_iota(jnp.int32, wide.shape, 1) // z.cols
            mine = owner == lax.broadcasted_iota(jnp.int32, wide.shape, 0)
            parts.append(jnp.where(mine, wide, 0.0))
        rows.append(jnp.concatenate(parts, 1))
    shape = (z.rows * z.col_tiles, z.lanes)
    source_at = lax.broadcasted_iota(jnp.int32, shape, 0)
    same_row = source_at // z.col_tiles == lane_group(z, shape, 0)
    same_col = source_at % z.cols == lane_group(z, shape, 1)
    expand = jnp.where(same_row & same_col, 1.0, 0.0).astype(F32)
    return finish_weights(z, rows[0], rows[1], expand)


def column_weights(z, here, ranks_ref, scales_ref, f):
    rows = []
    for source in (None, ranks_ref):
        parts = []
        for r in range(z.rows):
            at = pl.ds(r, z.tiles, stride=z.rows)
            if source is None:
                parts.append(scales_ref[f, 0, at, :] * scales_ref[f, 1, at, :])
            else:
                parts.append(ranks_ref[f, at, :].astype(F32))
        rows.append(jnp.concatenate(parts, 1))
    shape = (z.rows * z.col_tiles, z.lanes)
    source_at = lax.broadcasted_iota(jnp.int32, shape, 0)
    same_row = source_at // z.col_tiles == lane_group(z, shape, 0)
    same_col = source_at % z.col_tiles == z.cols * here + lane_group(z, shape, 1)
    expand = jnp.where(same_row & same_col, 1.0, 0.0).astype(F32)
    return finish_weights(z, rows[0], rows[1], expand)


def contract(z, block, ref, f, vectors, which, weights, out_ref):
    first = jnp.concatenate([x for re, im in vectors for x in (re, im)], 0).astype(BF16)
    second = jnp.concatenate([x for re, im in vectors for x in (im, -re)], 0).astype(BF16)
    high = 2 * z.virtual
    group = lane_group(z, (high, 2 * z.lanes), which)
    for pair in range(z.tiles // 2):
        total = lax.dot_general(
            first, block_pair(block, z, ref, f, 0, pair), NT, preferred_element_type=F32
        ) + lax.dot_general(
            second, block_pair(block, z, ref, f, 1, pair), NT, preferred_element_type=F32
        )
        picked = total[:high]
        for at in range(1, len(vectors)):
            picked = jnp.where(group == at, total[at * high : (at + 1) * high], picked)
        for half in range(2):
            s = 2 * pair + half
            part = picked[:, half * z.lanes : (half + 1) * z.lanes] * weights[s : s + 1]
            out_ref[s, f] = part.astype(BF16)


def combine(z, block, ref, f, arrived_ref, which, count):
    total = None
    v = z.virtual
    for pair in range(z.tiles // 2):
        coefs = jnp.concatenate([arrived_ref[2 * pair, f], arrived_ref[2 * pair + 1, f]], 1).astype(F32)
        turned = jnp.concatenate([-coefs[v:], coefs[:v]], 0)
        group = lane_group(z, coefs.shape, which)
        for c, rows in enumerate((coefs, turned)):
            masked = jnp.concatenate([jnp.where(group == at, rows, 0.0) for at in range(count)], 0)
            part = jnp.dot(
                masked.astype(BF16), block_pair(block, z, ref, f, c, pair), preferred_element_type=F32
            )
            total = part if total is None else total + part
    return total


def fetch(z, hbm, vmem, sems):
    copies = [pltpu.make_async_copy(hbm.at[f], vmem.at[f], sems.at[f]) for f in range(z.freqs)]
    for copy in copies:
        copy.start()
    return copies


def first_duals_kernel(z, left_hbm, recorded_ref, ranks_ref, scales_ref, out_ref, u, sems):
    copies = fetch(z, left_hbm, u, sems)
    here = lax.axis_index("tile")
    for f in range(z.freqs):
        weights = row_weights(z, here, ranks_ref, scales_ref, f)
        vectors = []
        for r in range(z.rows):
            at = slice(r * z.side, (r + 1) * z.side)
            vectors.append((recorded_ref[f, 0, :, at], recorded_ref[f, 1, :, at]))
        copies[f].wait()
        contract(z, left_block, u, f, vectors, 0, weights, out_ref)


def source_rows(z, f, c, j, half):
    halves = z.side // 128
    start = (j * halves + half) * z.pairs + 2 * f + c
    return pl.ds(start, z.virtual, stride=z.cols * halves * z.pairs)


def gradient_kernel(z, with_first, right_hbm, arrived_ref, steps_ref, *refs):
    if with_first:
        first_ref, out_ref, v, sems = refs
    else:
        out_ref, v, sems = refs
    copies = fetch(z, right_hbm, v, sems)
    high = 2 * z.virtual
    for f in range(z.freqs):
        copies[f].wait()
        total = combine(z, right_block, v, f, arrived_ref, 1, z.cols) * steps_ref[f]
        for j in range(z.cols):
            for c in range(2):
                start = j * high + c * z.virtual
                rows = total[start : start + z.virtual]
                for half in range(z.side // 128):
                    at = source_rows(z, f, c, j, half)
                    part = rows[:, half * 128 : (half + 1) * 128]
                    out_ref[at, :] = first_ref[at, :] + part if with_first else part


def threshold_kernel(z, arrived_ref, table_ref, thresholds_ref, out_ref):
    table = table_ref[...]
    halves = z.side // 128
    fields = [arrived_ref[:, half].reshape(z.times, 128) for half in range(halves)]
    signal = jnp.dot(table, jnp.concatenate(fields, 1), precision=HIGHEST, preferred_element_type=F32)
    level = thresholds_ref[lax.axis_index("freq") // z.cols]
    kept = signal - jnp.clip(signal, -level, level)
    back = lax.dot_general(
        table, kept, (((0,), (0,)), ((), ())), precision=HIGHEST, preferred_element_type=F32
    )
    for half in range(halves):
        out_ref[:, half] = back[:, half * 128 : (half + 1) * 128].reshape(z.groups, z.pairs, 128)


def field_rows(z, ref, f, c, j):
    return jnp.concatenate([ref[source_rows(z, f, c, j, half), :] for half in range(z.side // 128)], 1)


def coefficients_kernel(z, right_hbm, field_ref, ranks_ref, scales_ref, out_ref, v, sems):
    copies = fetch(z, right_hbm, v, sems)
    here = lax.axis_index("tile")
    for f in range(z.freqs):
        weights = column_weights(z, here, ranks_ref, scales_ref, f)
        vectors = [(field_rows(z, field_ref, f, 0, j), field_rows(z, field_ref, f, 1, j)) for j in range(z.cols)]
        copies[f].wait()
        contract(z, right_block, v, f, vectors, 1, weights, out_ref)


def residual_kernel(z, left_hbm, arrived_ref, recorded_ref, ranks_ref, scales_ref, out_ref, u, sems):
    copies = fetch(z, left_hbm, u, sems)
    here = lax.axis_index("tile")
    v = z.virtual
    for f in range(z.freqs):
        weights = row_weights(z, here, ranks_ref, scales_ref, f)
        copies[f].wait()
        image = combine(z, left_block, u, f, arrived_ref, 0, z.rows)
        vectors = []
        for r in range(z.rows):
            at = slice(r * z.side, (r + 1) * z.side)
            start = 2 * r * v
            vectors.append(
                (
                    recorded_ref[f, 0, :, at] - image[start : start + v],
                    recorded_ref[f, 1, :, at] - image[start + v : start + 2 * v],
                )
            )
        contract(z, left_block, u, f, vectors, 0, weights, out_ref)


def output_kernel(z, field_ref, out_ref):
    for f in range(z.freqs):
        for c in range(2):
            for j in range(z.cols):
                out_ref[f, c, :, j * z.side : (j + 1) * z.side] = field_rows(z, field_ref, f, c, j)


def dft_table(freqs, times):
    f = np.arange(freqs)[:, None]
    t = np.arange(times)[None, :]
    angles = ((f * t) % times) * (2.0 * math.pi / times)
    scaling = np.where(f == 0, math.sqrt(1.0 / times), math.sqrt(2.0 / times))
    both = np.stack([scaling * np.cos(angles), -scaling * np.sin(angles)], 1)
    return np.ascontiguousarray(both.reshape(2 * freqs, times).T.astype(np.float32))


HBM = pl.BlockSpec(memory_space=pl.ANY)
VMEM = pl.BlockSpec(memory_space=pltpu.VMEM)
SMEM = pl.BlockSpec(memory_space=pltpu.SMEM)


def run(name, kernel, in_specs, out, scratch=()):
    return pl.pallas_call(
        kernel,
        name=name,
        in_specs=in_specs,
        out_specs=VMEM,
        out_shape=out,
        scratch_shapes=list(scratch),
        interpret=INTERPRET,
        compiler_params=pltpu.CompilerParams(vmem_limit_bytes=40 << 20),
    )


def per_device(left, right, tile_ranks, tile_scales, recorded, step_sizes, thresholds, tiles, groups):
    z = Sizes(left, right, recorded, tiles, groups)
    held_left = [pltpu.VMEM(left.shape, BF16), pltpu.SemaphoreType.DMA((z.freqs,))]
    held_right = [pltpu.VMEM(right.shape, BF16), pltpu.SemaphoreType.DMA((z.freqs,))]
    coefs = jax.ShapeDtypeStruct((z.tiles, z.freqs, 2 * z.virtual, z.lanes), BF16)
    halves = z.side // 128
    rows = z.groups * halves * z.pairs
    field = jax.ShapeDtypeStruct((rows, 128), F32)
    blocks = jax.ShapeDtypeStruct((z.groups, halves, z.pairs, 128), F32)
    table = jnp.asarray(dft_table(z.freqs * z.groups, z.times))

    def over_tile(x):
        return lax.all_to_all(x, "tile", split_axis=0, concat_axis=0, tiled=True)

    def over_freq(x):
        return lax.all_to_all(x.reshape(blocks.shape), "freq", split_axis=0, concat_axis=0, tiled=True)

    part = functools.partial
    duals = run("first_duals", part(first_duals_kernel, z), [HBM, VMEM, VMEM, VMEM], coefs, held_left)(
        left, recorded, tile_ranks, tile_scales
    )
    update = run("first_gradient", part(gradient_kernel, z, False), [HBM, VMEM, SMEM], field, held_right)(
        right, over_tile(duals), step_sizes
    )
    shrink = run("threshold", part(threshold_kernel, z), [VMEM, VMEM, SMEM], blocks)
    first = over_freq(shrink(over_freq(update), table, thresholds)).reshape(rows, 128)
    coeffs = run("coefficients", part(coefficients_kernel, z), [HBM, VMEM, VMEM, VMEM], coefs, held_right)(
        right, first, tile_ranks, tile_scales
    )
    duals = run("residual", part(residual_kernel, z), [HBM, VMEM, VMEM, VMEM, VMEM], coefs, held_left)(
        left, over_tile(coeffs), recorded, tile_ranks, tile_scales
    )
    update = run("second_gradient", part(gradient_kernel, z, True), [HBM, VMEM, SMEM, VMEM], field, held_right)(
        right, over_tile(duals), step_sizes, first
    )
    second = over_freq(shrink(over_freq(update), table, thresholds)).reshape(rows, 128)
    out = jax.ShapeDtypeStruct((z.freqs, 2, z.virtual, z.cols * z.side), F32)
    return run("output", part(output_kernel, z), [VMEM], out)(second)


def solution(mesh):
    return jax.shard_map(
        functools.partial(per_device, tiles=mesh.shape["tile"], groups=mesh.shape["freq"]),
        mesh=mesh,
        in_specs=(
            P("freq", "tile", None, None, None, None),
            P("freq", None, "tile", None, None, None),
            P("freq", None, None),
            P("freq", None, None, None),
            P("freq", None, None, "tile"),
            P("freq"),
            P(),
        ),
        out_specs=P("freq", None, None, "tile"),
        check_vma=False,
    )
```

```python
import functools
import math

import jax
import jax.numpy as jnp
import ml_dtypes
import numpy as np
from jax import lax
from jax.experimental import pallas as pl
from jax.experimental.pallas import tpu as pltpu
from jax.sharding import PartitionSpec as P

F32 = jnp.float32
BF16 = jnp.bfloat16
HIGHEST = lax.Precision.HIGHEST
NT = (((1,), (1,)), ((), ()))
INTERPRET = False


class Sizes:
    def __init__(self, left, right, recorded, tiles, groups):
        self.freqs, self.rows, self.col_tiles, _, self.slots, self.side = left.shape
        self.row_tiles, self.cols = right.shape[1], right.shape[2]
        self.virtual = recorded.shape[2]
        self.tiles, self.groups = tiles, groups
        self.lanes = self.rows * self.cols * self.slots
        self.pairs = 2 * self.freqs
        self.times = 2 * self.freqs * groups
        assert self.lanes == 128 and self.virtual == 8 and self.tiles % 2 == 0
        assert self.groups == self.virtual * self.cols and self.slots == 16


def lane_group(z, shape, which):
    lane = lax.broadcasted_iota(jnp.int32, shape, 1) % z.lanes
    if which == 0:
        return lane // (z.cols * z.slots)
    return (lane // z.slots) % z.cols


def left_block(z, u, f, c, s):
    return u[f, :, z.cols * s : z.cols * (s + 1), c].reshape(z.lanes, z.side)


def right_block(z, v, f, c, s):
    return v[f, z.rows * s : z.rows * (s + 1), :, c].reshape(z.lanes, z.side)


def block_pair(block, z, ref, f, c, pair):
    return jnp.concatenate([block(z, ref, f, c, 2 * pair), block(z, ref, f, c, 2 * pair + 1)], 0)


def expand_weights(z, scales, ranks, expand):
    wide = jnp.dot(scales, expand, precision=HIGHEST, preferred_element_type=F32)
    live = jnp.dot(ranks.astype(BF16), expand.astype(BF16), preferred_element_type=F32)
    slot = (lax.broadcasted_iota(jnp.int32, wide.shape, 1) % z.slots).astype(F32)
    return jnp.where(slot < live, wide, 0.0)


def row_weights(z, here, ranks_ref, scales_ref):
    tables = []
    for scales in (True, False):
        rows = []
        for f in range(z.freqs):
            parts = []
            for r in range(z.rows):
                at = pl.ds(z.rows * here + r, 1)
                if scales:
                    one = scales_ref[f, 0, at, :] * scales_ref[f, 1, at, :]
                else:
                    one = ranks_ref[f, at, :].astype(F32)
                wide = jnp.broadcast_to(one, (z.tiles, z.col_tiles))
                owner = lax.broadcasted_iota(jnp.int32, wide.shape, 1) // z.cols
                mine = owner == lax.broadcasted_iota(jnp.int32, wide.shape, 0)
                parts.append(jnp.where(mine, wide, 0.0))
            rows.append(jnp.concatenate(parts, 1))
        tables.append(jnp.concatenate(rows, 0))
    shape = (z.rows * z.col_tiles, z.lanes)
    source_at = lax.broadcasted_iota(jnp.int32, shape, 0)
    same_row = source_at // z.col_tiles == lane_group(z, shape, 0)
    same_col = source_at % z.cols == lane_group(z, shape, 1)
    return expand_weights(z, *tables, jnp.where(same_row & same_col, 1.0, 0.0).astype(F32))


def column_weights(z, here, ranks_ref, scales_ref):
    tables = []
    for scales in (True, False):
        rows = []
        for f in range(z.freqs):
            parts = []
            for r in range(z.rows):
                at = pl.ds(r, z.tiles, stride=z.rows)
                if scales:
                    parts.append(scales_ref[f, 0, at, :] * scales_ref[f, 1, at, :])
                else:
                    parts.append(ranks_ref[f, at, :].astype(F32))
            rows.append(jnp.concatenate(parts, 1))
        tables.append(jnp.concatenate(rows, 0))
    shape = (z.rows * z.col_tiles, z.lanes)
    source_at = lax.broadcasted_iota(jnp.int32, shape, 0)
    same_row = source_at // z.col_tiles == lane_group(z, shape, 0)
    same_col = source_at % z.col_tiles == z.cols * here + lane_group(z, shape, 1)
    return expand_weights(z, *tables, jnp.where(same_row & same_col, 1.0, 0.0).astype(F32))


def contract(z, block, ref, f, vectors, which, weights_ref, out_ref):
    straight = jnp.concatenate([x for re, im in vectors for x in (re, im)], 0)
    turned = jnp.concatenate([x for re, im in vectors for x in (im, -re)], 0)
    both = jnp.concatenate([straight, turned], 1).astype(BF16)
    high = 2 * z.virtual
    group = lane_group(z, (high, 2 * z.lanes), which)
    for pair in range(z.tiles // 2):
        parts = [block_pair(block, z, ref, f, c, pair) for c in range(2)]
        total = lax.dot_general(both, jnp.concatenate(parts, 1), NT, preferred_element_type=F32)
        picked = total[:high]
        for at in range(1, len(vectors)):
            picked = jnp.where(group == at, total[at * high : (at + 1) * high], picked)
        for half in range(2):
            s = 2 * pair + half
            weight = weights_ref[f * z.tiles + s : f * z.tiles + s + 1, :]
            out_ref[s, f] = (picked[:, half * z.lanes : (half + 1) * z.lanes] * weight).astype(BF16)


def combine(z, block, ref, f, arrived_ref, which, count):
    total = None
    v = z.virtual
    for pair in range(z.tiles // 2):
        coefs = jnp.concatenate([arrived_ref[2 * pair, f], arrived_ref[2 * pair + 1, f]], 1).astype(F32)
        turned = jnp.concatenate([-coefs[v:], coefs[:v]], 0)
        group = lane_group(z, coefs.shape, which)
        sides = []
        for rows in (coefs, turned):
            sides.append(jnp.concatenate([jnp.where(group == at, rows, 0.0) for at in range(count)], 0))
        parts = [block_pair(block, z, ref, f, c, pair) for c in range(2)]
        part = jnp.dot(
            jnp.concatenate(sides, 1).astype(BF16), jnp.concatenate(parts, 0), preferred_element_type=F32
        )
        total = part if total is None else total + part
    return total


def first_duals_kernel(
    z, left_hbm, recorded_hbm, ranks_hbm, scales_hbm, steps_hbm, levels_hbm, out_ref, row_ref, col_ref, scalars_ref,
    u, recorded, ranks, scales, steps, levels, sems, small,
):
    here = lax.axis_index("tile")
    little = [
        pltpu.make_async_copy(source, target, small.at[n])
        for n, (source, target) in enumerate(
            (
                (ranks_hbm, ranks),
                (scales_hbm, scales),
                (recorded_hbm, recorded),
                (steps_hbm, steps),
                (levels_hbm, levels),
            )
        )
    ]
    wide = z.col_tiles // 4
    copies = [
        [
            pltpu.make_async_copy(
                left_hbm.at[f, r, pl.ds(q * wide, wide)], u.at[f, r, pl.ds(q * wide, wide)], sems.at[f, r, q]
            )
            for r in range(z.rows)
            for q in range(4)
        ]
        for f in range(z.freqs)
    ]
    for copy in little + [copy for group in copies for copy in group]:
        copy.start()
    little[0].wait()
    little[1].wait()
    row_ref[...] = row_weights(z, here, ranks, scales)
    col_ref[...] = column_weights(z, here, ranks, scales)
    for copy in little[2:]:
        copy.wait()
    at = lax.broadcasted_iota(jnp.int32, scalars_ref.shape, 0)
    scalars = jnp.full(scalars_ref.shape, levels[lax.axis_index("freq") // z.cols], F32)
    for f in range(z.freqs):
        scalars = jnp.where(at == f, steps[f], scalars)
    scalars_ref[...] = scalars
    for f in range(z.freqs):
        vectors = []
        for r in range(z.rows):
            at = slice(r * z.side, (r + 1) * z.side)
            vectors.append((recorded[f, 0, :, at], recorded[f, 1, :, at]))
        for copy in copies[f]:
            copy.wait()
        contract(z, left_block, u, f, vectors, 0, row_ref, out_ref)


def source_rows(z, f, c, j, half):
    halves = z.side // 128
    start = (j * halves + half) * z.pairs + 2 * f + c
    return pl.ds(start, z.virtual, stride=z.cols * halves * z.pairs)


def gradient(z, right, f, arrived_ref, scalars_ref, rows_ref):
    high = 2 * z.virtual
    total = combine(z, right_block, right, f, arrived_ref, 1, z.cols)
    for j in range(z.cols):
        for c in range(2):
            start = j * high + c * z.virtual
            for half in range(z.side // 128):
                part = total[start : start + z.virtual, half * 128 : (half + 1) * 128]
                rows_ref[source_rows(z, f, c, j, half), :] = part * scalars_ref[f : f + 1, :]


def first_gradient_kernel(z, right, arrived_ref, scalars_ref, out_ref):
    for f in range(z.freqs):
        gradient(z, right, f, arrived_ref, scalars_ref, out_ref)


def second_gradient_kernel(z, right, arrived_ref, scalars_ref, out_ref, rows_ref):
    for f in range(z.freqs):
        gradient(z, right, f, arrived_ref, scalars_ref, rows_ref)
    out_ref[...] = rows_ref[...].reshape(out_ref.shape).astype(BF16)


def times(tables_ref, which, x):
    high = x.astype(BF16)
    low = (x - high.astype(F32)).astype(BF16)
    return jnp.dot(tables_ref[which], jnp.concatenate([high, low, high], 0), preferred_element_type=F32)


def threshold(z, field, tables_ref, scalars_ref, out_ref):
    halves = z.side // 128
    signal = times(tables_ref, 0, field)
    level = jnp.concatenate([scalars_ref[z.freqs : z.freqs + 1, :]] * halves, 1)
    back = times(tables_ref, 1, signal - jnp.clip(signal, -level, level))
    parts = [back[:, half * 128 : (half + 1) * 128].reshape(z.groups, z.pairs, 128) for half in range(halves)]
    out_ref[...] = jnp.concatenate(parts, 1).astype(BF16)
    return back


def field_of(z, blocks):
    halves = z.side // 128
    parts = [blocks[:, half * z.pairs : (half + 1) * z.pairs].reshape(z.times, 128) for half in range(halves)]
    return jnp.concatenate(parts, 1)


def first_threshold_kernel(z, arrived_ref, tables_ref, scalars_ref, out_ref, first_ref):
    first_ref[...] = threshold(z, field_of(z, arrived_ref[...]), tables_ref, scalars_ref, out_ref)


def second_threshold_kernel(z, arrived_ref, first_ref, tables_ref, scalars_ref, out_ref):
    field = first_ref[...] + field_of(z, arrived_ref[...].astype(F32))
    threshold(z, field, tables_ref, scalars_ref, out_ref)


def field_rows(z, ref, f, c, j):
    return jnp.concatenate([ref[source_rows(z, f, c, j, half), :] for half in range(z.side // 128)], 1)


def coefficients_kernel(z, right, field_ref, weights_ref, out_ref, rows_ref):
    rows_ref[...] = field_ref[...].astype(F32).reshape(rows_ref.shape)
    for f in range(z.freqs):
        vectors = [(field_rows(z, rows_ref, f, 0, j), field_rows(z, rows_ref, f, 1, j)) for j in range(z.cols)]
        contract(z, right_block, right, f, vectors, 1, weights_ref, out_ref)


def residual_kernel(z, left, arrived_ref, recorded_ref, weights_ref, out_ref):
    v = z.virtual
    for f in range(z.freqs):
        image = combine(z, left_block, left, f, arrived_ref, 0, z.rows)
        vectors = []
        for r in range(z.rows):
            at = slice(r * z.side, (r + 1) * z.side)
            start = 2 * r * v
            vectors.append(
                (
                    recorded_ref[f, 0, :, at] - image[start : start + v],
                    recorded_ref[f, 1, :, at] - image[start + v : start + 2 * v],
                )
            )
        contract(z, left_block, left, f, vectors, 0, weights_ref, out_ref)


def output_kernel(z, field_ref, out_ref, rows_ref):
    rows_ref[...] = field_ref[...].astype(F32).reshape(rows_ref.shape)
    for f in range(z.freqs):
        for c in range(2):
            for j in range(z.cols):
                out_ref[f, c, :, j * z.side : (j + 1) * z.side] = field_rows(z, rows_ref, f, c, j)


def dft_tables(freqs, times):
    f = np.arange(freqs)[:, None]
    t = np.arange(times)[None, :]
    angles = ((f * t) % times) * (2.0 * math.pi / times)
    scaling = np.where(f == 0, math.sqrt(1.0 / times), math.sqrt(2.0 / times))
    both = np.stack([scaling * np.cos(angles), -scaling * np.sin(angles)], 1)
    forth = np.ascontiguousarray(both.reshape(2 * freqs, times).T.astype(np.float32))
    sides = []
    for table in (forth, forth.T):
        high = table.astype(ml_dtypes.bfloat16)
        low = (table - high.astype(np.float32)).astype(ml_dtypes.bfloat16)
        sides.append(np.concatenate([high, high, low], 1))
    return np.stack(sides)


HBM = pl.BlockSpec(memory_space=pltpu.HBM)
VMEM = pl.BlockSpec(memory_space=pltpu.VMEM)


def run(name, kernel, in_specs, out, scratch=()):
    return pl.pallas_call(
        kernel,
        name=name,
        in_specs=in_specs,
        out_specs=VMEM if isinstance(out, jax.ShapeDtypeStruct) else [VMEM] * len(out),
        out_shape=out,
        scratch_shapes=list(scratch),
        interpret=INTERPRET,
        compiler_params=pltpu.CompilerParams(vmem_limit_bytes=40 << 20),
    )


def per_device(left, right, tile_ranks, tile_scales, recorded, step_sizes, thresholds, tiles, groups):
    z = Sizes(left, right, recorded, tiles, groups)
    part = functools.partial
    shape = jax.ShapeDtypeStruct
    halves = z.side // 128
    coefs = shape((z.tiles, z.freqs, 2 * z.virtual, z.lanes), BF16)
    weights = shape((z.freqs * z.tiles, z.lanes), F32)
    rows = (z.groups * halves * z.pairs, 128)
    short = shape((z.groups, halves * z.pairs, 128), BF16)
    rows_scratch = [pltpu.VMEM(rows, F32)]
    tables = jnp.asarray(dft_tables(z.freqs * z.groups, z.times))

    def over_tile(x):
        return lax.all_to_all(x, "tile", split_axis=0, concat_axis=0, tiled=True)

    def over_freq(x):
        return lax.all_to_all(x, "freq", split_axis=0, concat_axis=0, tiled=True)

    def far(x):
        return pltpu.with_memory_space_constraint(x, pltpu.HBM)

    held = [pltpu.VMEM(x.shape, x.dtype) for x in (left, recorded, tile_ranks, tile_scales)]
    held += [pltpu.SMEM(x.shape, x.dtype) for x in (step_sizes, thresholds)]
    held += [pltpu.SemaphoreType.DMA((z.freqs, z.rows, 4)), pltpu.SemaphoreType.DMA((5,))]
    duals, row_weight, col_weight, scalars = run(
        "first_duals", part(first_duals_kernel, z), [HBM] * 6, [coefs, weights, weights, shape((8, 128), F32)], held
    )(far(left), far(recorded), far(tile_ranks), far(tile_scales), far(step_sizes), far(thresholds))
    update = run("first_gradient", part(first_gradient_kernel, z), [VMEM] * 3, shape(rows, F32))(
        right, over_tile(duals), scalars
    )
    sent, first = run(
        "first_threshold", part(first_threshold_kernel, z), [VMEM] * 3, [short, shape((z.times, z.side), F32)]
    )(over_freq(update.reshape(z.groups, halves * z.pairs, 128)), tables, scalars)
    coeffs = run("coefficients", part(coefficients_kernel, z), [VMEM] * 3, coefs, rows_scratch)(
        right, over_freq(sent), col_weight
    )
    duals = run("residual", part(residual_kernel, z), [VMEM] * 4, coefs)(
        left, over_tile(coeffs), recorded, row_weight
    )
    update = run("second_gradient", part(second_gradient_kernel, z), [VMEM] * 3, short, rows_scratch)(
        right, over_tile(duals), scalars
    )
    sent = run("second_threshold", part(second_threshold_kernel, z), [VMEM] * 4, short)(
        over_freq(update), first, tables, scalars
    )
    out = shape((z.freqs, 2, z.virtual, z.cols * z.side), F32)
    return run("output", part(output_kernel, z), [VMEM], out, rows_scratch)(over_freq(sent))


def solution(mesh):
    return jax.shard_map(
        functools.partial(per_device, tiles=mesh.shape["tile"], groups=mesh.shape["freq"]),
        mesh=mesh,
        in_specs=(
            P("freq", "tile", None, None, None, None),
            P("freq", None, "tile", None, None, None),
            P("freq", None, None),
            P("freq", None, None, None),
            P("freq", None, None, "tile"),
            P("freq"),
            P(),
        ),
        out_specs=P("freq", None, None, "tile"),
        check_vma=False,
    )
```

```python
import functools
import math

import jax
import jax.numpy as jnp
import ml_dtypes
import numpy as np
from jax import lax
from jax.experimental import pallas as pl
from jax.experimental.pallas import tpu as pltpu
from jax.sharding import PartitionSpec as P

F32 = jnp.float32
BF16 = jnp.bfloat16
HIGHEST = lax.Precision.HIGHEST
NT = (((1,), (1,)), ((), ()))
INTERPRET = False


class Sizes:
    def __init__(self, left, right, recorded, tiles, groups):
        self.freqs, self.rows, self.col_tiles, _, self.slots, self.side = left.shape
        self.row_tiles, self.cols = right.shape[1], right.shape[2]
        self.virtual = recorded.shape[2]
        self.tiles, self.groups = tiles, groups
        self.lanes = self.rows * self.cols * self.slots
        self.pairs = 2 * self.freqs
        self.times = 2 * self.freqs * groups
        assert self.lanes == 128 and self.virtual == 8 and self.tiles % 2 == 0
        assert self.groups == self.virtual * self.cols and self.slots == 16


def lane_group(z, shape, which):
    lane = lax.broadcasted_iota(jnp.int32, shape, 1) % z.lanes
    if which == 0:
        return lane // (z.cols * z.slots)
    return (lane // z.slots) % z.cols


def left_block(z, u, f, c, s):
    return u[f, :, z.cols * s : z.cols * (s + 1), c].reshape(z.lanes, z.side)


def right_block(z, v, f, c, s):
    return v[f, z.rows * s : z.rows * (s + 1), :, c].reshape(z.lanes, z.side)


def block_pair(block, z, ref, f, c, pair):
    return jnp.concatenate([block(z, ref, f, c, 2 * pair), block(z, ref, f, c, 2 * pair + 1)], 0)


def expand_weights(z, scales, ranks, expand):
    terms, rest = [], scales
    for _ in range(3):
        terms.append(rest.astype(BF16).astype(F32))
        rest = rest - terms[-1]
    zero = jnp.zeros_like(ranks)
    left = jnp.concatenate([jnp.concatenate(terms, 1), jnp.concatenate([ranks, zero, zero], 1)], 0)
    wide = jnp.dot(left.astype(BF16), jnp.concatenate([expand] * 3, 0).astype(BF16), preferred_element_type=F32)
    count = scales.shape[0]
    slot = (lax.broadcasted_iota(jnp.int32, (count, z.lanes), 1) % z.slots).astype(F32)
    return jnp.where(slot < wide[count:], wide[:count], 0.0)


def row_weights(z, here, ranks_ref, scales_ref):
    tables = []
    for scales in (True, False):
        rows = []
        for f in range(z.freqs):
            parts = []
            for r in range(z.rows):
                at = pl.ds(z.rows * here + r, 1)
                if scales:
                    one = scales_ref[f, 0, at, :] * scales_ref[f, 1, at, :]
                else:
                    one = ranks_ref[f, at, :].astype(F32)
                wide = jnp.broadcast_to(one, (z.tiles, z.col_tiles))
                owner = lax.broadcasted_iota(jnp.int32, wide.shape, 1) // z.cols
                mine = owner == lax.broadcasted_iota(jnp.int32, wide.shape, 0)
                parts.append(jnp.where(mine, wide, 0.0))
            rows.append(jnp.concatenate(parts, 1))
        tables.append(jnp.concatenate(rows, 0))
    shape = (z.rows * z.col_tiles, z.lanes)
    source_at = lax.broadcasted_iota(jnp.int32, shape, 0)
    same_row = source_at // z.col_tiles == lane_group(z, shape, 0)
    same_col = source_at % z.cols == lane_group(z, shape, 1)
    return expand_weights(z, *tables, jnp.where(same_row & same_col, 1.0, 0.0).astype(F32))


def column_weights(z, here, ranks_ref, scales_ref):
    tables = []
    for scales in (True, False):
        rows = []
        for f in range(z.freqs):
            parts = []
            for r in range(z.rows):
                at = pl.ds(r, z.tiles, stride=z.rows)
                if scales:
                    parts.append(scales_ref[f, 0, at, :] * scales_ref[f, 1, at, :])
                else:
                    parts.append(ranks_ref[f, at, :].astype(F32))
            rows.append(jnp.concatenate(parts, 1))
        tables.append(jnp.concatenate(rows, 0))
    shape = (z.rows * z.col_tiles, z.lanes)
    source_at = lax.broadcasted_iota(jnp.int32, shape, 0)
    same_row = source_at // z.col_tiles == lane_group(z, shape, 0)
    same_col = source_at % z.col_tiles == z.cols * here + lane_group(z, shape, 1)
    return expand_weights(z, *tables, jnp.where(same_row & same_col, 1.0, 0.0).astype(F32))


def contract(z, block, ref, f, vectors, which, weights_ref, out_ref):
    straight = jnp.concatenate([x for re, im in vectors for x in (re, im)], 0)
    turned = jnp.concatenate([x for re, im in vectors for x in (im, -re)], 0)
    both = jnp.concatenate([straight, turned], 1).astype(BF16)
    high = 2 * z.virtual
    group = lane_group(z, (high, 2 * z.lanes), which)
    for pair in range(z.tiles // 2):
        parts = [block_pair(block, z, ref, f, c, pair) for c in range(2)]
        total = lax.dot_general(both, jnp.concatenate(parts, 1), NT, preferred_element_type=F32)
        picked = total[:high]
        for at in range(1, len(vectors)):
            picked = jnp.where(group == at, total[at * high : (at + 1) * high], picked)
        for half in range(2):
            s = 2 * pair + half
            weight = weights_ref[f * z.tiles + s : f * z.tiles + s + 1, :]
            out_ref[s, f] = (picked[:, half * z.lanes : (half + 1) * z.lanes] * weight).astype(BF16)


def combine(z, block, ref, f, arrived_ref, which, count):
    total = None
    v = z.virtual
    for pair in range(z.tiles // 2):
        coefs = jnp.concatenate([arrived_ref[2 * pair, f], arrived_ref[2 * pair + 1, f]], 1).astype(F32)
        turned = jnp.concatenate([-coefs[v:], coefs[:v]], 0)
        group = lane_group(z, coefs.shape, which)
        sides = []
        for rows in (coefs, turned):
            sides.append(jnp.concatenate([jnp.where(group == at, rows, 0.0) for at in range(count)], 0))
        parts = [block_pair(block, z, ref, f, c, pair) for c in range(2)]
        part = jnp.dot(
            jnp.concatenate(sides, 1).astype(BF16), jnp.concatenate(parts, 0), preferred_element_type=F32
        )
        total = part if total is None else total + part
    return total


def first_duals_kernel(
    z, left_hbm, recorded_hbm, ranks_hbm, scales_hbm, steps_hbm, levels_hbm, out_ref, row_ref, col_ref, scalars_ref,
    u, recorded, ranks, scales, steps, levels, sems, small,
):
    here = lax.axis_index("tile")
    little = [
        pltpu.make_async_copy(source, target, small.at[n])
        for n, (source, target) in enumerate(
            (
                (ranks_hbm, ranks),
                (scales_hbm, scales),
                (recorded_hbm, recorded),
                (steps_hbm, steps),
                (levels_hbm, levels),
            )
        )
    ]
    copies = [pltpu.make_async_copy(left_hbm.at[f], u.at[f], sems.at[f]) for f in range(z.freqs)]
    for copy in little + copies:
        copy.start()
    little[0].wait()
    little[1].wait()
    row_ref[...] = row_weights(z, here, ranks, scales)
    col_ref[...] = column_weights(z, here, ranks, scales)
    little[2].wait()
    for f in range(z.freqs):
        vectors = []
        for r in range(z.rows):
            at = slice(r * z.side, (r + 1) * z.side)
            vectors.append((recorded[f, 0, :, at], recorded[f, 1, :, at]))
        copies[f].wait()
        contract(z, left_block, u, f, vectors, 0, row_ref, out_ref)
    little[3].wait()
    little[4].wait()
    at = lax.broadcasted_iota(jnp.int32, scalars_ref.shape, 0)
    scalars = jnp.full(scalars_ref.shape, levels[lax.axis_index("freq") // z.cols], F32)
    for f in range(z.freqs):
        scalars = jnp.where(at == f, steps[f], scalars)
    scalars_ref[...] = scalars


def source_rows(z, f, c, j, half):
    halves = z.side // 128
    start = (j * halves + half) * z.pairs + 2 * f + c
    return pl.ds(start, z.virtual, stride=z.cols * halves * z.pairs)


def gradient(z, right, f, arrived_ref, scalars_ref, rows_ref):
    high = 2 * z.virtual
    total = combine(z, right_block, right, f, arrived_ref, 1, z.cols)
    for j in range(z.cols):
        for c in range(2):
            start = j * high + c * z.virtual
            for half in range(z.side // 128):
                part = total[start : start + z.virtual, half * 128 : (half + 1) * 128]
                rows_ref[source_rows(z, f, c, j, half), :] = part * scalars_ref[f : f + 1, :]


def first_gradient_kernel(z, right, arrived_ref, scalars_ref, out_ref):
    for f in range(z.freqs):
        gradient(z, right, f, arrived_ref, scalars_ref, out_ref)


def second_gradient_kernel(z, right, arrived_ref, scalars_ref, out_ref, rows_ref):
    for f in range(z.freqs):
        gradient(z, right, f, arrived_ref, scalars_ref, rows_ref)
    out_ref[...] = rows_ref[...].reshape(out_ref.shape).astype(BF16)


def times(tables_ref, which, x):
    high = x.astype(BF16)
    low = (x - high.astype(F32)).astype(BF16)
    return jnp.dot(tables_ref[which], jnp.concatenate([high, low, high], 0), preferred_element_type=F32)


def threshold(z, field, tables_ref, scalars_ref, out_ref):
    halves = z.side // 128
    signal = times(tables_ref, 0, field)
    level = jnp.concatenate([scalars_ref[z.freqs : z.freqs + 1, :]] * halves, 1)
    back = times(tables_ref, 1, signal - jnp.clip(signal, -level, level))
    parts = [back[:, half * 128 : (half + 1) * 128].reshape(z.groups, z.pairs, 128) for half in range(halves)]
    out_ref[...] = jnp.concatenate(parts, 1).astype(BF16)
    return back


def field_of(z, blocks):
    halves = z.side // 128
    parts = [blocks[:, half * z.pairs : (half + 1) * z.pairs].reshape(z.times, 128) for half in range(halves)]
    return jnp.concatenate(parts, 1)


def first_threshold_kernel(z, arrived_ref, tables_ref, scalars_ref, out_ref, first_ref):
    first_ref[...] = threshold(z, field_of(z, arrived_ref[...]), tables_ref, scalars_ref, out_ref)


def second_threshold_kernel(z, arrived_ref, first_ref, tables_ref, scalars_ref, out_ref):
    field = first_ref[...] + field_of(z, arrived_ref[...].astype(F32))
    threshold(z, field, tables_ref, scalars_ref, out_ref)


def field_rows(z, ref, f, c, j):
    return jnp.concatenate([ref[source_rows(z, f, c, j, half), :] for half in range(z.side // 128)], 1)


def coefficients_kernel(z, right, field_ref, weights_ref, out_ref, rows_ref):
    rows_ref[...] = field_ref[...].astype(F32).reshape(rows_ref.shape)
    for f in range(z.freqs):
        vectors = [(field_rows(z, rows_ref, f, 0, j), field_rows(z, rows_ref, f, 1, j)) for j in range(z.cols)]
        contract(z, right_block, right, f, vectors, 1, weights_ref, out_ref)


def residual_kernel(z, left, arrived_ref, recorded_ref, weights_ref, out_ref):
    v = z.virtual
    images = [combine(z, left_block, left, f, arrived_ref, 0, z.rows) for f in range(z.freqs)]
    for f, image in enumerate(images):
        vectors = []
        for r in range(z.rows):
            at = slice(r * z.side, (r + 1) * z.side)
            start = 2 * r * v
            vectors.append(
                (
                    recorded_ref[f, 0, :, at] - image[start : start + v],
                    recorded_ref[f, 1, :, at] - image[start + v : start + 2 * v],
                )
            )
        contract(z, left_block, left, f, vectors, 0, weights_ref, out_ref)


def output_kernel(z, field_ref, out_hbm, rows_ref, held, sems):
    rows_ref[...] = field_ref[...].astype(F32).reshape(rows_ref.shape)
    copies = []
    for f in range(z.freqs):
        for c in range(2):
            for j in range(z.cols):
                held[f, c, :, j * z.side : (j + 1) * z.side] = field_rows(z, rows_ref, f, c, j)
        copies.append(pltpu.make_async_copy(held.at[f], out_hbm.at[f], sems.at[f]))
        copies[f].start()
    for copy in copies:
        copy.wait()


def dft_tables(freqs, times):
    f = np.arange(freqs)[:, None]
    t = np.arange(times)[None, :]
    angles = ((f * t) % times) * (2.0 * math.pi / times)
    scaling = np.where(f == 0, math.sqrt(1.0 / times), math.sqrt(2.0 / times))
    both = np.stack([scaling * np.cos(angles), -scaling * np.sin(angles)], 1)
    forth = np.ascontiguousarray(both.reshape(2 * freqs, times).T.astype(np.float32))
    sides = []
    for table in (forth, forth.T):
        high = table.astype(ml_dtypes.bfloat16)
        low = (table - high.astype(np.float32)).astype(ml_dtypes.bfloat16)
        sides.append(np.concatenate([high, high, low], 1))
    return np.stack(sides)


HBM = pl.BlockSpec(memory_space=pltpu.HBM)
VMEM = pl.BlockSpec(memory_space=pltpu.VMEM)


def run(name, kernel, in_specs, out, scratch=(), out_specs=VMEM, cost=None):
    return pl.pallas_call(
        kernel,
        name=name,
        in_specs=in_specs,
        out_specs=out_specs if isinstance(out, jax.ShapeDtypeStruct) else [out_specs] * len(out),
        out_shape=out,
        scratch_shapes=list(scratch),
        interpret=INTERPRET,
        cost_estimate=cost,
        compiler_params=pltpu.CompilerParams(vmem_limit_bytes=40 << 20),
    )


def per_device(left, right, tile_ranks, tile_scales, recorded, step_sizes, thresholds, tiles, groups):
    z = Sizes(left, right, recorded, tiles, groups)
    part = functools.partial
    shape = jax.ShapeDtypeStruct
    halves = z.side // 128
    coefs = shape((z.tiles, z.freqs, 2 * z.virtual, z.lanes), BF16)
    weights = shape((z.freqs * z.tiles, z.lanes), F32)
    rows = (z.groups * halves * z.pairs, 128)
    short = shape((z.groups, halves * z.pairs, 128), BF16)
    rows_scratch = [pltpu.VMEM(rows, F32)]
    tables = jnp.asarray(dft_tables(z.freqs * z.groups, z.times))

    def over_tile(x):
        return lax.all_to_all(x, "tile", split_axis=0, concat_axis=0, tiled=True)

    def over_freq(x):
        return lax.all_to_all(x, "freq", split_axis=0, concat_axis=0, tiled=True)

    def far(x):
        return pltpu.with_memory_space_constraint(x, pltpu.HBM)

    held = [pltpu.VMEM(x.shape, x.dtype) for x in (left, recorded, tile_ranks, tile_scales)]
    held += [pltpu.SMEM(x.shape, x.dtype) for x in (step_sizes, thresholds)]
    held += [pltpu.SemaphoreType.DMA((z.freqs,)), pltpu.SemaphoreType.DMA((5,))]
    duals, row_weight, col_weight, scalars = run(
        "first_duals", part(first_duals_kernel, z), [HBM] * 6, [coefs, weights, weights, shape((8, 128), F32)], held
    )(far(left), far(recorded), far(tile_ranks), far(tile_scales), far(step_sizes), far(thresholds))
    update = run("first_gradient", part(first_gradient_kernel, z), [VMEM] * 3, shape(rows, F32))(
        right, over_tile(duals), scalars
    )
    sent, first = run(
        "first_threshold", part(first_threshold_kernel, z), [VMEM] * 3, [short, shape((z.times, z.side), F32)]
    )(over_freq(update.reshape(z.groups, halves * z.pairs, 128)), tables, scalars)
    coeffs = run("coefficients", part(coefficients_kernel, z), [VMEM] * 3, coefs, rows_scratch)(
        right, over_freq(sent), col_weight
    )
    duals = run("residual", part(residual_kernel, z), [VMEM] * 4, coefs)(
        left, over_tile(coeffs), recorded, row_weight
    )
    update = run("second_gradient", part(second_gradient_kernel, z), [VMEM] * 3, short, rows_scratch)(
        right, over_tile(duals), scalars
    )
    sent = run("second_threshold", part(second_threshold_kernel, z), [VMEM] * 4, short)(
        over_freq(update), first, tables, scalars
    )
    out = shape((z.freqs, 2, z.virtual, z.cols * z.side), F32)
    held = rows_scratch + [pltpu.VMEM(out.shape, F32), pltpu.SemaphoreType.DMA((z.freqs,))]
    return run("output", part(output_kernel, z), [VMEM], out, held, HBM)(over_freq(sent))


def solution(mesh):
    return jax.shard_map(
        functools.partial(per_device, tiles=mesh.shape["tile"], groups=mesh.shape["freq"]),
        mesh=mesh,
        in_specs=(
            P("freq", "tile", None, None, None, None),
            P("freq", None, "tile", None, None, None),
            P("freq", None, None),
            P("freq", None, None, None),
            P("freq", None, None, "tile"),
            P("freq"),
            P(),
        ),
        out_specs=P("freq", None, None, "tile"),
        check_vma=False,
    )
```

```python
import functools
import math

import jax
import jax.numpy as jnp
import ml_dtypes
import numpy as np
from jax import lax
from jax.experimental import pallas as pl
from jax.experimental.pallas import tpu as pltpu
from jax.sharding import PartitionSpec as P

F32 = jnp.float32
BF16 = jnp.bfloat16
HIGHEST = lax.Precision.HIGHEST
NT = (((1,), (1,)), ((), ()))
KNEE = 0.25
INTERPRET = False


class Sizes:
    def __init__(self, left, right, recorded, tiles, groups):
        self.freqs, self.rows, self.col_tiles, _, self.slots, self.side = left.shape
        self.row_tiles, self.cols = right.shape[1], right.shape[2]
        self.virtual = recorded.shape[2]
        self.tiles, self.groups = tiles, groups
        self.team = groups // 2
        self.lanes = self.rows * self.cols * self.slots
        self.pairs = 2 * self.freqs
        self.times = 2 * self.freqs * groups
        assert self.lanes == 128 and self.virtual == 8 and self.tiles % 2 == 0
        assert self.groups == self.virtual * self.cols and self.cols % 2 == 0 and self.slots == 16


def lane_group(z, shape, which):
    lane = lax.broadcasted_iota(jnp.int32, shape, 1) % z.lanes
    if which == 0:
        return lane // (z.cols * z.slots)
    return (lane // z.slots) % z.cols


def left_block(z, u, f, c, s):
    return u[f, :, z.cols * s : z.cols * (s + 1), c].reshape(z.lanes, z.side)


def right_block(z, v, f, c, s):
    return v[f, z.rows * s : z.rows * (s + 1), :, c].reshape(z.lanes, z.side)


def block_pair(block, z, ref, f, c, pair):
    return jnp.concatenate([block(z, ref, f, c, 2 * pair), block(z, ref, f, c, 2 * pair + 1)], 0)


def expand_weights(z, scales, ranks, expand):
    terms, rest = [], scales
    for _ in range(3):
        terms.append(rest.astype(BF16).astype(F32))
        rest = rest - terms[-1]
    zero = jnp.zeros_like(ranks)
    left = jnp.concatenate([jnp.concatenate(terms, 1), jnp.concatenate([ranks, zero, zero], 1)], 0)
    wide = jnp.dot(left.astype(BF16), jnp.concatenate([expand] * 3, 0).astype(BF16), preferred_element_type=F32)
    count = scales.shape[0]
    slot = (lax.broadcasted_iota(jnp.int32, (count, z.lanes), 1) % z.slots).astype(F32)
    return jnp.where(slot < wide[count:], wide[:count], 0.0)


def row_weights(z, here, ranks_ref, scales_ref):
    tables = []
    for scales in (True, False):
        rows = []
        for f in range(z.freqs):
            parts = []
            for r in range(z.rows):
                at = pl.ds(z.rows * here + r, 1)
                if scales:
                    one = scales_ref[f, 0, at, :] * scales_ref[f, 1, at, :]
                else:
                    one = ranks_ref[f, at, :].astype(F32)
                wide = jnp.broadcast_to(one, (z.tiles, z.col_tiles))
                owner = lax.broadcasted_iota(jnp.int32, wide.shape, 1) // z.cols
                mine = owner == lax.broadcasted_iota(jnp.int32, wide.shape, 0)
                parts.append(jnp.where(mine, wide, 0.0))
            rows.append(jnp.concatenate(parts, 1))
        tables.append(jnp.concatenate(rows, 0))
    shape = (z.rows * z.col_tiles, z.lanes)
    source_at = lax.broadcasted_iota(jnp.int32, shape, 0)
    same_row = source_at // z.col_tiles == lane_group(z, shape, 0)
    same_col = source_at % z.cols == lane_group(z, shape, 1)
    return expand_weights(z, *tables, jnp.where(same_row & same_col, 1.0, 0.0).astype(F32))


def column_weights(z, here, ranks_ref, scales_ref):
    tables = []
    for scales in (True, False):
        rows = []
        for f in range(z.freqs):
            parts = []
            for r in range(z.rows):
                at = pl.ds(r, z.tiles, stride=z.rows)
                if scales:
                    parts.append(scales_ref[f, 0, at, :] * scales_ref[f, 1, at, :])
                else:
                    parts.append(ranks_ref[f, at, :].astype(F32))
            rows.append(jnp.concatenate(parts, 1))
        tables.append(jnp.concatenate(rows, 0))
    shape = (z.rows * z.col_tiles, z.lanes)
    source_at = lax.broadcasted_iota(jnp.int32, shape, 0)
    same_row = source_at // z.col_tiles == lane_group(z, shape, 0)
    same_col = source_at % z.col_tiles == z.cols * here + lane_group(z, shape, 1)
    return expand_weights(z, *tables, jnp.where(same_row & same_col, 1.0, 0.0).astype(F32))


def contract(z, block, ref, f, vectors, which, weights_ref, out_ref):
    straight = jnp.concatenate([x for re, im in vectors for x in (re, im)], 0)
    turned = jnp.concatenate([x for re, im in vectors for x in (im, -re)], 0)
    both = jnp.concatenate([straight, turned], 1).astype(BF16)
    high = 2 * z.virtual
    group = lane_group(z, (high, 2 * z.lanes), which)
    for pair in range(z.tiles // 2):
        parts = [block_pair(block, z, ref, f, c, pair) for c in range(2)]
        total = lax.dot_general(both, jnp.concatenate(parts, 1), NT, preferred_element_type=F32)
        picked = total[:high]
        for at in range(1, len(vectors)):
            picked = jnp.where(group == at, total[at * high : (at + 1) * high], picked)
        for half in range(2):
            s = 2 * pair + half
            weight = weights_ref[f * z.tiles + s : f * z.tiles + s + 1, :]
            out_ref[s, f] = (picked[:, half * z.lanes : (half + 1) * z.lanes] * weight).astype(BF16)


def combine(z, block, ref, f, arrived_ref, which, count):
    total = None
    v = z.virtual
    for pair in range(z.tiles // 2):
        coefs = jnp.concatenate([arrived_ref[2 * pair, f], arrived_ref[2 * pair + 1, f]], 1).astype(F32)
        turned = jnp.concatenate([-coefs[v:], coefs[:v]], 0)
        group = lane_group(z, coefs.shape, which)
        sides = []
        for rows in (coefs, turned):
            sides.append(jnp.concatenate([jnp.where(group == at, rows, 0.0) for at in range(count)], 0))
        parts = [block_pair(block, z, ref, f, c, pair) for c in range(2)]
        part = jnp.dot(
            jnp.concatenate(sides, 1).astype(BF16), jnp.concatenate(parts, 0), preferred_element_type=F32
        )
        total = part if total is None else total + part
    return total


def first_duals_kernel(
    z, left_hbm, recorded_hbm, ranks_hbm, scales_hbm, steps_hbm, levels_hbm, out_ref, row_ref, col_ref, scalars_ref,
    u, recorded, ranks, scales, steps, levels, sems, small,
):
    here = lax.axis_index("tile")
    little = [
        pltpu.make_async_copy(source, target, small.at[n])
        for n, (source, target) in enumerate(
            (
                (ranks_hbm, ranks),
                (scales_hbm, scales),
                (recorded_hbm, recorded),
                (steps_hbm, steps),
                (levels_hbm, levels),
            )
        )
    ]
    copies = [pltpu.make_async_copy(left_hbm.at[f], u.at[f], sems.at[f]) for f in range(z.freqs)]
    for copy in little + copies:
        copy.start()
    little[0].wait()
    little[1].wait()
    row_ref[...] = row_weights(z, here, ranks, scales)
    col_ref[...] = column_weights(z, here, ranks, scales)
    little[2].wait()
    for f in range(z.freqs):
        vectors = []
        for r in range(z.rows):
            at = slice(r * z.side, (r + 1) * z.side)
            vectors.append((recorded[f, 0, :, at], recorded[f, 1, :, at]))
        copies[f].wait()
        contract(z, left_block, u, f, vectors, 0, row_ref, out_ref)
    little[3].wait()
    little[4].wait()
    at = lax.broadcasted_iota(jnp.int32, scalars_ref.shape, 0)
    scalars = jnp.full(scalars_ref.shape, levels[lax.axis_index("freq") % z.team // (z.team // z.virtual)], F32)
    for f in range(z.freqs):
        scalars = jnp.where(at == f, steps[f], scalars)
    scalars_ref[...] = scalars


def source_rows(z, f, c, j, half):
    halves = z.side // 128
    start = (j * halves + half) * z.pairs + 2 * f + c
    return pl.ds(start, z.virtual, stride=z.cols * halves * z.pairs)


def gradient(z, right, f, arrived_ref, scalars_ref, rows_ref):
    high = 2 * z.virtual
    total = combine(z, right_block, right, f, arrived_ref, 1, z.cols)
    for j in range(z.cols):
        for c in range(2):
            start = j * high + c * z.virtual
            for half in range(z.side // 128):
                part = total[start : start + z.virtual, half * 128 : (half + 1) * 128]
                rows_ref[source_rows(z, f, c, j, half), :] = part * scalars_ref[f : f + 1, :]


def encode(x):
    w = jnp.abs(x) * (1.0 / KNEE)
    t = w + jnp.sqrt(w * w + 1.0)
    square = t * t
    fifth = square * square * t * 2.0**-60
    return jnp.where(x < 0.0, -fifth * fifth, fifth * fifth).astype(BF16)


def decode(code):
    z = code.astype(F32)
    t = jnp.exp((jnp.log(jnp.abs(z)) + 120.0 * math.log(2.0)) * 0.1)
    size = (t - 1.0 / t) * (0.5 * KNEE)
    return jnp.where(z < 0.0, -size, size)


def send_twice(z, blocks, out_ref):
    for team in range(2):
        out_ref[team * z.team : (team + 1) * z.team] = blocks


def first_gradient_kernel(z, right, arrived_ref, scalars_ref, out_ref, rows_ref):
    for f in range(z.freqs):
        gradient(z, right, f, arrived_ref, scalars_ref, rows_ref)
    send_twice(z, encode(rows_ref[...].reshape(z.team, -1, 128)), out_ref)


def second_gradient_kernel(z, right, arrived_ref, scalars_ref, out_ref, rows_ref):
    for f in range(z.freqs):
        gradient(z, right, f, arrived_ref, scalars_ref, rows_ref)
    send_twice(z, rows_ref[...].reshape(z.team, -1, 128).astype(BF16), out_ref)


def times(table, x):
    high = x.astype(BF16)
    low = (x - high.astype(F32)).astype(BF16)
    return jnp.dot(table, jnp.concatenate([high, low, high], 0), preferred_element_type=F32)


def threshold(z, field, tables_ref, scalars_ref):
    signal = times(tables_ref[0], field)
    level = jnp.concatenate([scalars_ref[z.freqs : z.freqs + 1, :]] * (field.shape[1] // 128), 1)
    return signal - jnp.clip(signal, -level, level)


def send_back(z, mine, out_ref):
    parts = [
        mine[:, lo : lo + 128].reshape(z.team, z.pairs, 128) for lo in range(0, mine.shape[1], 128)
    ]
    out_ref[...] = jnp.concatenate(parts, 1).astype(BF16)


def field_of(z, blocks):
    parts = [
        blocks[:, lo : lo + z.pairs].reshape(z.times, 128) for lo in range(0, blocks.shape[1], z.pairs)
    ]
    return jnp.concatenate(parts, 1)


def team_rows(z):
    count = z.team * z.pairs
    return pl.ds(pl.multiple_of(lax.axis_index("freq") // z.team * count, count), count)


def first_threshold_kernel(z, arrived_ref, tables_ref, scalars_ref, out_ref, first_ref):
    kept = threshold(z, field_of(z, decode(arrived_ref[...])), tables_ref, scalars_ref)
    first_ref[...] = times(tables_ref[1], kept)
    send_back(z, first_ref[team_rows(z), :], out_ref)


def second_threshold_kernel(z, arrived_ref, first_ref, tables_ref, scalars_ref, out_ref):
    field = first_ref[...] + field_of(z, arrived_ref[...].astype(F32))
    kept = threshold(z, field, tables_ref, scalars_ref)
    send_back(z, times(tables_ref[1, team_rows(z), :], kept), out_ref)


def field_rows(z, ref, f, c, j):
    return jnp.concatenate([ref[source_rows(z, f, c, j, half), :] for half in range(z.side // 128)], 1)


def coefficients_kernel(z, right, field_ref, weights_ref, out_ref, rows_ref):
    rows_ref[...] = field_ref[...].astype(F32).reshape(rows_ref.shape)
    for f in range(z.freqs):
        vectors = [(field_rows(z, rows_ref, f, 0, j), field_rows(z, rows_ref, f, 1, j)) for j in range(z.cols)]
        contract(z, right_block, right, f, vectors, 1, weights_ref, out_ref)


def residual_kernel(z, left, arrived_ref, recorded_ref, weights_ref, out_ref):
    v = z.virtual
    images = [combine(z, left_block, left, f, arrived_ref, 0, z.rows) for f in range(z.freqs)]
    for f, image in enumerate(images):
        vectors = []
        for r in range(z.rows):
            at = slice(r * z.side, (r + 1) * z.side)
            start = 2 * r * v
            vectors.append(
                (
                    recorded_ref[f, 0, :, at] - image[start : start + v],
                    recorded_ref[f, 1, :, at] - image[start + v : start + 2 * v],
                )
            )
        contract(z, left_block, left, f, vectors, 0, weights_ref, out_ref)


def output_kernel(z, field_ref, out_hbm, rows_ref, held, sems):
    rows_ref[...] = field_ref[...].astype(F32).reshape(rows_ref.shape)
    copies = []
    for f in range(z.freqs):
        for c in range(2):
            for j in range(z.cols):
                held[f, c, :, j * z.side : (j + 1) * z.side] = field_rows(z, rows_ref, f, c, j)
        copies.append(pltpu.make_async_copy(held.at[f], out_hbm.at[f], sems.at[f]))
        copies[f].start()
    for copy in copies:
        copy.wait()


def dft_tables(freqs, times):
    f = np.arange(freqs)[:, None]
    t = np.arange(times)[None, :]
    angles = ((f * t) % times) * (2.0 * math.pi / times)
    scaling = np.where(f == 0, math.sqrt(1.0 / times), math.sqrt(2.0 / times))
    both = np.stack([scaling * np.cos(angles), -scaling * np.sin(angles)], 1)
    forth = np.ascontiguousarray(both.reshape(2 * freqs, times).T.astype(np.float32))
    sides = []
    for table in (forth, forth.T):
        high = table.astype(ml_dtypes.bfloat16)
        low = (table - high.astype(np.float32)).astype(ml_dtypes.bfloat16)
        sides.append(np.concatenate([high, high, low], 1))
    return np.stack(sides)


HBM = pl.BlockSpec(memory_space=pltpu.HBM)
VMEM = pl.BlockSpec(memory_space=pltpu.VMEM)


def run(name, kernel, in_specs, out, scratch=(), out_specs=VMEM, cost=None):
    return pl.pallas_call(
        kernel,
        name=name,
        in_specs=in_specs,
        out_specs=out_specs if isinstance(out, jax.ShapeDtypeStruct) else [out_specs] * len(out),
        out_shape=out,
        scratch_shapes=list(scratch),
        interpret=INTERPRET,
        cost_estimate=cost,
        compiler_params=pltpu.CompilerParams(vmem_limit_bytes=40 << 20),
    )


def per_device(left, right, tile_ranks, tile_scales, recorded, step_sizes, thresholds, tiles, groups):
    z = Sizes(left, right, recorded, tiles, groups)
    part = functools.partial
    shape = jax.ShapeDtypeStruct
    halves = z.side // 128
    coefs = shape((z.tiles, z.freqs, 2 * z.virtual, z.lanes), BF16)
    weights = shape((z.freqs * z.tiles, z.lanes), F32)
    rows = (z.groups * halves * z.pairs, 128)
    forth = shape((z.groups, 2 * halves * z.pairs, 128), BF16)
    back = shape((z.team, 2 * halves * z.pairs, 128), BF16)
    teams = [list(range(at, at + z.team)) for at in (0, z.team)]
    rows_scratch = [pltpu.VMEM(rows, F32)]
    tables = jnp.asarray(dft_tables(z.freqs * z.groups, z.times))

    def over_tile(x):
        return lax.all_to_all(x, "tile", split_axis=0, concat_axis=0, tiled=True)

    def over_freq(x):
        return lax.all_to_all(x, "freq", split_axis=0, concat_axis=0, tiled=True)

    def over_team(x):
        return lax.all_to_all(x, "freq", split_axis=0, concat_axis=0, tiled=True, axis_index_groups=teams)

    def far(x):
        return pltpu.with_memory_space_constraint(x, pltpu.HBM)

    held = [pltpu.VMEM(x.shape, x.dtype) for x in (left, recorded, tile_ranks, tile_scales)]
    held += [pltpu.SMEM(x.shape, x.dtype) for x in (step_sizes, thresholds)]
    held += [pltpu.SemaphoreType.DMA((z.freqs,)), pltpu.SemaphoreType.DMA((5,))]
    duals, row_weight, col_weight, scalars = run(
        "first_duals", part(first_duals_kernel, z), [HBM] * 6, [coefs, weights, weights, shape((8, 128), F32)], held
    )(far(left), far(recorded), far(tile_ranks), far(tile_scales), far(step_sizes), far(thresholds))
    update = run("first_gradient", part(first_gradient_kernel, z), [VMEM] * 3, forth, rows_scratch)(
        right, over_tile(duals), scalars
    )
    sent, first = run(
        "first_threshold", part(first_threshold_kernel, z), [VMEM] * 3, [back, shape((z.times, 2 * z.side), F32)]
    )(over_freq(update), tables, scalars)
    coeffs = run("coefficients", part(coefficients_kernel, z), [VMEM] * 3, coefs, rows_scratch)(
        right, over_team(sent), col_weight
    )
    duals = run("residual", part(residual_kernel, z), [VMEM] * 4, coefs)(
        left, over_tile(coeffs), recorded, row_weight
    )
    update = run("second_gradient", part(second_gradient_kernel, z), [VMEM] * 3, forth, rows_scratch)(
        right, over_tile(duals), scalars
    )
    sent = run("second_threshold", part(second_threshold_kernel, z), [VMEM] * 4, back)(
        over_freq(update), first, tables, scalars
    )
    out = shape((z.freqs, 2, z.virtual, z.cols * z.side), F32)
    held = rows_scratch + [pltpu.VMEM(out.shape, F32), pltpu.SemaphoreType.DMA((z.freqs,))]
    return run("output", part(output_kernel, z), [VMEM], out, held, HBM)(over_team(sent))


def solution(mesh):
    return jax.shard_map(
        functools.partial(per_device, tiles=mesh.shape["tile"], groups=mesh.shape["freq"]),
        mesh=mesh,
        in_specs=(
            P("freq", "tile", None, None, None, None),
            P("freq", None, "tile", None, None, None),
            P("freq", None, None),
            P("freq", None, None, None),
            P("freq", None, None, "tile"),
            P("freq"),
            P(),
        ),
        out_specs=P("freq", None, None, "tile"),
        check_vma=False,
    )
```

```python
import functools
import math

import jax
import jax.numpy as jnp
import ml_dtypes
import numpy as np
from jax import lax
from jax.experimental import pallas as pl
from jax.experimental.pallas import tpu as pltpu
from jax.sharding import PartitionSpec as P

F32 = jnp.float32
BF16 = jnp.bfloat16
HIGHEST = lax.Precision.HIGHEST
NT = (((1,), (1,)), ((), ()))
KNEE = 0.25
INTERPRET = False


class Sizes:
    def __init__(self, left, right, recorded, tiles, groups):
        self.freqs, self.rows, self.col_tiles, _, self.slots, self.side = left.shape
        self.row_tiles, self.cols = right.shape[1], right.shape[2]
        self.virtual = recorded.shape[2]
        self.tiles, self.groups = tiles, groups
        self.team = groups // 2
        self.lanes = self.rows * self.cols * self.slots
        self.pairs = 2 * self.freqs
        self.times = 2 * self.freqs * groups
        assert self.lanes == 128 and self.virtual == 8 and self.tiles % 2 == 0
        assert self.groups == self.virtual * self.cols and self.cols % 2 == 0 and self.slots == 16


def lane_group(z, shape, which):
    lane = lax.broadcasted_iota(jnp.int32, shape, 1) % z.lanes
    if which == 0:
        return lane // (z.cols * z.slots)
    return (lane // z.slots) % z.cols


def left_block(z, u, f, c, s):
    return u[f, :, z.cols * s : z.cols * (s + 1), c].reshape(z.lanes, z.side)


def right_block(z, v, f, c, s):
    return v[f, z.rows * s : z.rows * (s + 1), :, c].reshape(z.lanes, z.side)


def block_pair(block, z, ref, f, c, pair):
    return jnp.concatenate([block(z, ref, f, c, 2 * pair), block(z, ref, f, c, 2 * pair + 1)], 0)


def expand_weights(z, scales, ranks, expand):
    terms, rest = [], scales
    for _ in range(3):
        terms.append(rest.astype(BF16).astype(F32))
        rest = rest - terms[-1]
    zero = jnp.zeros_like(ranks)
    left = jnp.concatenate([jnp.concatenate(terms, 1), jnp.concatenate([ranks, zero, zero], 1)], 0)
    wide = jnp.dot(left.astype(BF16), jnp.concatenate([expand] * 3, 0).astype(BF16), preferred_element_type=F32)
    count = scales.shape[0]
    slot = (lax.broadcasted_iota(jnp.int32, (count, z.lanes), 1) % z.slots).astype(F32)
    return jnp.where(slot < wide[count:], wide[:count], 0.0)


def row_weights(z, here, ranks_ref, scales_ref):
    tables = []
    for scales in (True, False):
        rows = []
        for f in range(z.freqs):
            parts = []
            for r in range(z.rows):
                at = pl.ds(z.rows * here + r, 1)
                if scales:
                    one = scales_ref[f, 0, at, :] * scales_ref[f, 1, at, :]
                else:
                    one = ranks_ref[f, at, :].astype(F32)
                wide = jnp.broadcast_to(one, (z.tiles, z.col_tiles))
                owner = lax.broadcasted_iota(jnp.int32, wide.shape, 1) // z.cols
                mine = owner == lax.broadcasted_iota(jnp.int32, wide.shape, 0)
                parts.append(jnp.where(mine, wide, 0.0))
            rows.append(jnp.concatenate(parts, 1))
        tables.append(jnp.concatenate(rows, 0))
    shape = (z.rows * z.col_tiles, z.lanes)
    source_at = lax.broadcasted_iota(jnp.int32, shape, 0)
    same_row = source_at // z.col_tiles == lane_group(z, shape, 0)
    same_col = source_at % z.cols == lane_group(z, shape, 1)
    return expand_weights(z, *tables, jnp.where(same_row & same_col, 1.0, 0.0).astype(F32))


def column_weights(z, here, ranks_ref, scales_ref):
    tables = []
    for scales in (True, False):
        rows = []
        for f in range(z.freqs):
            parts = []
            for r in range(z.rows):
                at = pl.ds(r, z.tiles, stride=z.rows)
                if scales:
                    parts.append(scales_ref[f, 0, at, :] * scales_ref[f, 1, at, :])
                else:
                    parts.append(ranks_ref[f, at, :].astype(F32))
            rows.append(jnp.concatenate(parts, 1))
        tables.append(jnp.concatenate(rows, 0))
    shape = (z.rows * z.col_tiles, z.lanes)
    source_at = lax.broadcasted_iota(jnp.int32, shape, 0)
    same_row = source_at // z.col_tiles == lane_group(z, shape, 0)
    same_col = source_at % z.col_tiles == z.cols * here + lane_group(z, shape, 1)
    return expand_weights(z, *tables, jnp.where(same_row & same_col, 1.0, 0.0).astype(F32))


def contract(z, block, ref, f, vectors, which, weights_ref, out_ref):
    straight = jnp.concatenate([x for re, im in vectors for x in (re, im)], 0)
    turned = jnp.concatenate([x for re, im in vectors for x in (im, -re)], 0)
    both = jnp.concatenate([straight, turned], 1).astype(BF16)
    high = 2 * z.virtual
    group = lane_group(z, (high, 2 * z.lanes), which)
    for pair in range(z.tiles // 2):
        parts = [block_pair(block, z, ref, f, c, pair) for c in range(2)]
        total = lax.dot_general(both, jnp.concatenate(parts, 1), NT, preferred_element_type=F32)
        picked = total[:high]
        for at in range(1, len(vectors)):
            picked = jnp.where(group == at, total[at * high : (at + 1) * high], picked)
        for half in range(2):
            s = 2 * pair + half
            weight = weights_ref[f * z.tiles + s : f * z.tiles + s + 1, :]
            out_ref[s, f] = (picked[:, half * z.lanes : (half + 1) * z.lanes] * weight).astype(BF16)


def combine(z, block, ref, f, arrived_ref, which, count):
    total = None
    v = z.virtual
    for pair in range(z.tiles // 2):
        coefs = jnp.concatenate([arrived_ref[2 * pair, f], arrived_ref[2 * pair + 1, f]], 1).astype(F32)
        turned = jnp.concatenate([-coefs[v:], coefs[:v]], 0)
        group = lane_group(z, coefs.shape, which)
        sides = []
        for rows in (coefs, turned):
            sides.append(jnp.concatenate([jnp.where(group == at, rows, 0.0) for at in range(count)], 0))
        parts = [block_pair(block, z, ref, f, c, pair) for c in range(2)]
        part = jnp.dot(
            jnp.concatenate(sides, 1).astype(BF16), jnp.concatenate(parts, 0), preferred_element_type=F32
        )
        total = part if total is None else total + part
    return total


def first_duals_kernel(
    z, left_hbm, recorded_hbm, ranks_hbm, scales_hbm, steps_hbm, levels_hbm, out_ref, row_ref, col_ref, scalars_ref,
    u, recorded, ranks, scales, steps, levels, sems, small,
):
    here = lax.axis_index("tile")
    little = [
        pltpu.make_async_copy(source, target, small.at[n])
        for n, (source, target) in enumerate(
            (
                (ranks_hbm, ranks),
                (scales_hbm, scales),
                (recorded_hbm, recorded),
                (steps_hbm, steps),
                (levels_hbm, levels),
            )
        )
    ]
    copies = [pltpu.make_async_copy(left_hbm.at[f], u.at[f], sems.at[f]) for f in range(z.freqs)]
    for copy in little + copies:
        copy.start()
    little[0].wait()
    little[1].wait()
    row_ref[...] = row_weights(z, here, ranks, scales)
    col_ref[...] = column_weights(z, here, ranks, scales)
    little[2].wait()
    for f in range(z.freqs):
        vectors = []
        for r in range(z.rows):
            at = slice(r * z.side, (r + 1) * z.side)
            vectors.append((recorded[f, 0, :, at], recorded[f, 1, :, at]))
        copies[f].wait()
        contract(z, left_block, u, f, vectors, 0, row_ref, out_ref)
    little[3].wait()
    little[4].wait()
    at = lax.broadcasted_iota(jnp.int32, scalars_ref.shape, 0)
    scalars = jnp.full(scalars_ref.shape, levels[lax.axis_index("freq") % z.team // (z.team // z.virtual)], F32)
    for f in range(z.freqs):
        scalars = jnp.where(at == f, steps[f], scalars)
    scalars_ref[...] = scalars


def source_rows(z, f, c, j, half):
    halves = z.side // 128
    start = (j * halves + half) * z.pairs + 2 * f + c
    return pl.ds(start, z.virtual, stride=padded(z))


def padded(z):
    return z.cols * (z.side // 128) * z.pairs + 8


def spread_rows(z, blocks, rows_ref):
    held = padded(z) - 8
    rows = blocks.astype(F32).reshape(z.virtual * held, 128)
    for v in range(z.virtual):
        rows_ref[v * padded(z) : v * padded(z) + held, :] = rows[v * held : (v + 1) * held]


def gather_rows(z, rows_ref):
    held = padded(z) - 8
    rows = [rows_ref[v * padded(z) : v * padded(z) + held, :] for v in range(z.virtual)]
    return jnp.concatenate(rows, 0).reshape(z.team, -1, 128)


def gradient(z, right, f, arrived_ref, scalars_ref, rows_ref):
    high = 2 * z.virtual
    total = combine(z, right_block, right, f, arrived_ref, 1, z.cols)
    for j in range(z.cols):
        for c in range(2):
            start = j * high + c * z.virtual
            for half in range(z.side // 128):
                part = total[start : start + z.virtual, half * 128 : (half + 1) * 128]
                rows_ref[source_rows(z, f, c, j, half), :] = part * scalars_ref[f : f + 1, :]


def encode(x):
    w = jnp.abs(x) * (1.0 / KNEE)
    t = w + jnp.sqrt(w * w + 1.0)
    square = t * t
    fifth = square * square * t * 2.0**-60
    return jnp.where(x < 0.0, -fifth * fifth, fifth * fifth).astype(BF16)


def decode(code):
    z = code.astype(F32)
    t = jnp.exp((jnp.log(jnp.abs(z)) + 120.0 * math.log(2.0)) * 0.1)
    size = (t - 1.0 / t) * (0.5 * KNEE)
    return jnp.where(z < 0.0, -size, size)


def send_twice(z, blocks, out_ref):
    for team in range(2):
        out_ref[team * z.team : (team + 1) * z.team] = blocks


def first_gradient_kernel(z, right, arrived_ref, scalars_ref, out_ref, rows_ref):
    for f in range(z.freqs):
        gradient(z, right, f, arrived_ref, scalars_ref, rows_ref)
    send_twice(z, encode(gather_rows(z, rows_ref)), out_ref)


def second_gradient_kernel(z, right, arrived_ref, scalars_ref, out_ref, rows_ref):
    for f in range(z.freqs):
        gradient(z, right, f, arrived_ref, scalars_ref, rows_ref)
    send_twice(z, gather_rows(z, rows_ref).astype(BF16), out_ref)


def times(table, x):
    high = x.astype(BF16)
    low = (x - high.astype(F32)).astype(BF16)
    return jnp.dot(table, jnp.concatenate([high, low, high], 0), preferred_element_type=F32)


def threshold(z, field, tables_ref, scalars_ref):
    signal = times(tables_ref[0], field)
    level = jnp.concatenate([scalars_ref[z.freqs : z.freqs + 1, :]] * (field.shape[1] // 128), 1)
    return signal - jnp.clip(signal, -level, level)


def send_back(z, mine, out_ref):
    parts = [
        mine[:, lo : lo + 128].reshape(z.team, z.pairs, 128) for lo in range(0, mine.shape[1], 128)
    ]
    out_ref[...] = jnp.concatenate(parts, 1).astype(BF16)


def field_of(z, blocks):
    parts = [
        blocks[:, lo : lo + z.pairs].reshape(z.times, 128) for lo in range(0, blocks.shape[1], z.pairs)
    ]
    return jnp.concatenate(parts, 1)


def team_rows(z):
    count = z.team * z.pairs
    return pl.ds(pl.multiple_of(lax.axis_index("freq") // z.team * count, count), count)


def first_threshold_kernel(z, arrived_ref, tables_ref, scalars_ref, out_ref, first_ref):
    kept = threshold(z, field_of(z, decode(arrived_ref[...])), tables_ref, scalars_ref)
    first_ref[...] = times(tables_ref[1], kept)
    send_back(z, first_ref[team_rows(z), :], out_ref)


def second_threshold_kernel(z, arrived_ref, first_ref, tables_ref, scalars_ref, out_ref):
    field = first_ref[...] + field_of(z, arrived_ref[...].astype(F32))
    kept = threshold(z, field, tables_ref, scalars_ref)
    send_back(z, times(tables_ref[1, team_rows(z), :], kept), out_ref)


def field_rows(z, ref, f, c, j):
    return jnp.concatenate([ref[source_rows(z, f, c, j, half), :] for half in range(z.side // 128)], 1)


def coefficients_kernel(z, right, field_ref, weights_ref, out_ref, rows_ref):
    spread_rows(z, field_ref[...], rows_ref)
    for f in range(z.freqs):
        vectors = [(field_rows(z, rows_ref, f, 0, j), field_rows(z, rows_ref, f, 1, j)) for j in range(z.cols)]
        contract(z, right_block, right, f, vectors, 1, weights_ref, out_ref)


def residual_kernel(z, left, arrived_ref, recorded_ref, weights_ref, out_ref):
    v = z.virtual
    images = [combine(z, left_block, left, f, arrived_ref, 0, z.rows) for f in range(z.freqs)]
    for f, image in enumerate(images):
        vectors = []
        for r in range(z.rows):
            at = slice(r * z.side, (r + 1) * z.side)
            start = 2 * r * v
            vectors.append(
                (
                    recorded_ref[f, 0, :, at] - image[start : start + v],
                    recorded_ref[f, 1, :, at] - image[start + v : start + 2 * v],
                )
            )
        contract(z, left_block, left, f, vectors, 0, weights_ref, out_ref)


def output_kernel(z, field_ref, out_hbm, rows_ref, held, sems):
    spread_rows(z, field_ref[...], rows_ref)
    copies = []
    for f in range(z.freqs):
        for c in range(2):
            for j in range(z.cols):
                held[f, c, :, j * z.side : (j + 1) * z.side] = field_rows(z, rows_ref, f, c, j)
        copies.append(pltpu.make_async_copy(held.at[f], out_hbm.at[f], sems.at[f]))
        copies[f].start()
    for copy in copies:
        copy.wait()


def dft_tables(freqs, times):
    f = np.arange(freqs)[:, None]
    t = np.arange(times)[None, :]
    angles = ((f * t) % times) * (2.0 * math.pi / times)
    scaling = np.where(f == 0, math.sqrt(1.0 / times), math.sqrt(2.0 / times))
    both = np.stack([scaling * np.cos(angles), -scaling * np.sin(angles)], 1)
    forth = np.ascontiguousarray(both.reshape(2 * freqs, times).T.astype(np.float32))
    sides = []
    for table in (forth, forth.T):
        high = table.astype(ml_dtypes.bfloat16)
        low = (table - high.astype(np.float32)).astype(ml_dtypes.bfloat16)
        sides.append(np.concatenate([high, high, low], 1))
    return np.stack(sides)


HBM = pl.BlockSpec(memory_space=pltpu.HBM)
VMEM = pl.BlockSpec(memory_space=pltpu.VMEM)


def run(name, kernel, in_specs, out, scratch=(), out_specs=VMEM, cost=None):
    return pl.pallas_call(
        kernel,
        name=name,
        in_specs=in_specs,
        out_specs=out_specs if isinstance(out, jax.ShapeDtypeStruct) else [out_specs] * len(out),
        out_shape=out,
        scratch_shapes=list(scratch),
        interpret=INTERPRET,
        cost_estimate=cost,
        compiler_params=pltpu.CompilerParams(vmem_limit_bytes=40 << 20),
    )


def per_device(left, right, tile_ranks, tile_scales, recorded, step_sizes, thresholds, tiles, groups):
    z = Sizes(left, right, recorded, tiles, groups)
    part = functools.partial
    shape = jax.ShapeDtypeStruct
    halves = z.side // 128
    coefs = shape((z.tiles, z.freqs, 2 * z.virtual, z.lanes), BF16)
    weights = shape((z.freqs * z.tiles, z.lanes), F32)
    rows = (z.virtual * padded(z), 128)
    forth = shape((z.groups, 2 * halves * z.pairs, 128), BF16)
    back = shape((z.team, 2 * halves * z.pairs, 128), BF16)
    teams = [list(range(at, at + z.team)) for at in (0, z.team)]
    rows_scratch = [pltpu.VMEM(rows, F32)]
    tables = jnp.asarray(dft_tables(z.freqs * z.groups, z.times))

    def over_tile(x):
        return lax.all_to_all(x, "tile", split_axis=0, concat_axis=0, tiled=True)

    def over_freq(x):
        return lax.all_to_all(x, "freq", split_axis=0, concat_axis=0, tiled=True)

    def over_team(x):
        return lax.all_to_all(x, "freq", split_axis=0, concat_axis=0, tiled=True, axis_index_groups=teams)

    def far(x):
        return pltpu.with_memory_space_constraint(x, pltpu.HBM)

    held = [pltpu.VMEM(x.shape, x.dtype) for x in (left, recorded, tile_ranks, tile_scales)]
    held += [pltpu.SMEM(x.shape, x.dtype) for x in (step_sizes, thresholds)]
    held += [pltpu.SemaphoreType.DMA((z.freqs,)), pltpu.SemaphoreType.DMA((5,))]
    duals, row_weight, col_weight, scalars = run(
        "first_duals", part(first_duals_kernel, z), [HBM] * 6, [coefs, weights, weights, shape((8, 128), F32)], held
    )(far(left), far(recorded), far(tile_ranks), far(tile_scales), far(step_sizes), far(thresholds))
    update = run("first_gradient", part(first_gradient_kernel, z), [VMEM] * 3, forth, rows_scratch)(
        right, over_tile(duals), scalars
    )
    sent, first = run(
        "first_threshold", part(first_threshold_kernel, z), [VMEM] * 3, [back, shape((z.times, 2 * z.side), F32)]
    )(over_freq(update), tables, scalars)
    coeffs = run("coefficients", part(coefficients_kernel, z), [VMEM] * 3, coefs, rows_scratch)(
        right, over_team(sent), col_weight
    )
    duals = run("residual", part(residual_kernel, z), [VMEM] * 4, coefs)(
        left, over_tile(coeffs), recorded, row_weight
    )
    update = run("second_gradient", part(second_gradient_kernel, z), [VMEM] * 3, forth, rows_scratch)(
        right, over_tile(duals), scalars
    )
    sent = run("second_threshold", part(second_threshold_kernel, z), [VMEM] * 4, back)(
        over_freq(update), first, tables, scalars
    )
    out = shape((z.freqs, 2, z.virtual, z.cols * z.side), F32)
    held = rows_scratch + [pltpu.VMEM(out.shape, F32), pltpu.SemaphoreType.DMA((z.freqs,))]
    return run("output", part(output_kernel, z), [VMEM], out, held, HBM)(over_team(sent))


def solution(mesh):
    return jax.shard_map(
        functools.partial(per_device, tiles=mesh.shape["tile"], groups=mesh.shape["freq"]),
        mesh=mesh,
        in_specs=(
            P("freq", "tile", None, None, None, None),
            P("freq", None, "tile", None, None, None),
            P("freq", None, None),
            P("freq", None, None, None),
            P("freq", None, None, "tile"),
            P("freq"),
            P(),
        ),
        out_specs=P("freq", None, None, "tile"),
        check_vma=False,
    )
```

```python
import functools
import math

import jax
import jax.numpy as jnp
import ml_dtypes
import numpy as np
from jax import lax
from jax.experimental import pallas as pl
from jax.experimental.pallas import tpu as pltpu
from jax.sharding import PartitionSpec as P

F32 = jnp.float32
BF16 = jnp.bfloat16
HIGHEST = lax.Precision.HIGHEST
NT = (((1,), (1,)), ((), ()))
KNEE = 0.25
INTERPRET = False


class Sizes:
    def __init__(self, left, right, recorded, tiles, groups):
        self.freqs, self.rows, self.col_tiles, _, self.slots, self.side = left.shape
        self.row_tiles, self.cols = right.shape[1], right.shape[2]
        self.virtual = recorded.shape[2]
        self.tiles, self.groups = tiles, groups
        self.team = groups // 2
        self.lanes = self.rows * self.cols * self.slots
        self.pairs = 2 * self.freqs
        self.times = 2 * self.freqs * groups
        assert self.lanes == 128 and self.virtual == 8 and self.tiles % 2 == 0
        assert self.groups == self.virtual * self.cols and self.cols % 2 == 0 and self.slots == 16


def lane_group(z, shape, which):
    lane = lax.broadcasted_iota(jnp.int32, shape, 1) % z.lanes
    if which == 0:
        return lane // (z.cols * z.slots)
    return (lane // z.slots) % z.cols


def left_block(z, u, f, c, s):
    return u[f, :, z.cols * s : z.cols * (s + 1), c].reshape(z.lanes, z.side)


def right_block(z, v, f, c, s):
    return v[f, z.rows * s : z.rows * (s + 1), :, c].reshape(z.lanes, z.side)


def block_pair(block, z, ref, f, c, pair):
    return jnp.concatenate([block(z, ref, f, c, 2 * pair), block(z, ref, f, c, 2 * pair + 1)], 0)


def expand_weights(z, scales, ranks, expand):
    terms, rest = [], scales
    for _ in range(3):
        terms.append(rest.astype(BF16).astype(F32))
        rest = rest - terms[-1]
    zero = jnp.zeros_like(ranks)
    left = jnp.concatenate([jnp.concatenate(terms, 1), jnp.concatenate([ranks, zero, zero], 1)], 0)
    wide = jnp.dot(left.astype(BF16), jnp.concatenate([expand] * 3, 0).astype(BF16), preferred_element_type=F32)
    count = scales.shape[0]
    slot = (lax.broadcasted_iota(jnp.int32, (count, z.lanes), 1) % z.slots).astype(F32)
    return jnp.where(slot < wide[count:], wide[:count], 0.0)


def row_weights(z, here, ranks_ref, scales_ref):
    tables = []
    for scales in (True, False):
        rows = []
        for f in range(z.freqs):
            parts = []
            for r in range(z.rows):
                at = pl.ds(z.rows * here + r, 1)
                if scales:
                    one = scales_ref[f, 0, at, :] * scales_ref[f, 1, at, :]
                else:
                    one = ranks_ref[f, at, :].astype(F32)
                wide = jnp.broadcast_to(one, (z.tiles, z.col_tiles))
                owner = lax.broadcasted_iota(jnp.int32, wide.shape, 1) // z.cols
                mine = owner == lax.broadcasted_iota(jnp.int32, wide.shape, 0)
                parts.append(jnp.where(mine, wide, 0.0))
            rows.append(jnp.concatenate(parts, 1))
        tables.append(jnp.concatenate(rows, 0))
    shape = (z.rows * z.col_tiles, z.lanes)
    source_at = lax.broadcasted_iota(jnp.int32, shape, 0)
    same_row = source_at // z.col_tiles == lane_group(z, shape, 0)
    same_col = source_at % z.cols == lane_group(z, shape, 1)
    return expand_weights(z, *tables, jnp.where(same_row & same_col, 1.0, 0.0).astype(F32))


def column_weights(z, here, ranks_ref, scales_ref):
    tables = []
    for scales in (True, False):
        rows = []
        for f in range(z.freqs):
            parts = []
            for r in range(z.rows):
                at = pl.ds(r, z.tiles, stride=z.rows)
                if scales:
                    parts.append(scales_ref[f, 0, at, :] * scales_ref[f, 1, at, :])
                else:
                    parts.append(ranks_ref[f, at, :].astype(F32))
            rows.append(jnp.concatenate(parts, 1))
        tables.append(jnp.concatenate(rows, 0))
    shape = (z.rows * z.col_tiles, z.lanes)
    source_at = lax.broadcasted_iota(jnp.int32, shape, 0)
    same_row = source_at // z.col_tiles == lane_group(z, shape, 0)
    same_col = source_at % z.col_tiles == z.cols * here + lane_group(z, shape, 1)
    return expand_weights(z, *tables, jnp.where(same_row & same_col, 1.0, 0.0).astype(F32))


def contract(z, block, ref, f, vectors, which, weights_ref, out_ref):
    straight = jnp.concatenate([x for re, im in vectors for x in (re, im)], 0)
    turned = jnp.concatenate([x for re, im in vectors for x in (im, -re)], 0)
    both = jnp.concatenate([straight, turned], 1).astype(BF16)
    high = 2 * z.virtual
    group = lane_group(z, (high, 2 * z.lanes), which)
    for pair in range(z.tiles // 2):
        parts = [block_pair(block, z, ref, f, c, pair) for c in range(2)]
        total = lax.dot_general(both, jnp.concatenate(parts, 1), NT, preferred_element_type=F32)
        picked = total[:high]
        for at in range(1, len(vectors)):
            picked = jnp.where(group == at, total[at * high : (at + 1) * high], picked)
        for half in range(2):
            s = 2 * pair + half
            weight = weights_ref[f * z.tiles + s : f * z.tiles + s + 1, :]
            out_ref[s, f] = (picked[:, half * z.lanes : (half + 1) * z.lanes] * weight).astype(BF16)


def combine(z, block, ref, f, arrived_ref, which, count):
    lefts, rights = [], []
    v = z.virtual
    for pair in range(z.tiles // 2):
        coefs = jnp.concatenate([arrived_ref[2 * pair, f], arrived_ref[2 * pair + 1, f]], 1).astype(F32)
        turned = jnp.concatenate([-coefs[v:], coefs[:v]], 0)
        group = lane_group(z, coefs.shape, which)
        sides = []
        for rows in (coefs, turned):
            sides.append(jnp.concatenate([jnp.where(group == at, rows, 0.0) for at in range(count)], 0))
        parts = [block_pair(block, z, ref, f, c, pair) for c in range(2)]
        lefts += sides
        rights += parts
    return jnp.dot(
        jnp.concatenate(lefts, 1).astype(BF16), jnp.concatenate(rights, 0), preferred_element_type=F32
    )


def first_duals_kernel(
    z, left_hbm, recorded_hbm, ranks_hbm, scales_hbm, steps_hbm, levels_hbm, out_ref, row_ref, col_ref, scalars_ref,
    u, recorded, ranks, scales, steps, levels, sems, small,
):
    here = lax.axis_index("tile")
    little = [
        pltpu.make_async_copy(source, target, small.at[n])
        for n, (source, target) in enumerate(
            (
                (ranks_hbm, ranks),
                (scales_hbm, scales),
                (recorded_hbm, recorded),
                (steps_hbm, steps),
                (levels_hbm, levels),
            )
        )
    ]
    copies = [pltpu.make_async_copy(left_hbm.at[f], u.at[f], sems.at[f]) for f in range(z.freqs)]
    for copy in little + copies:
        copy.start()
    little[0].wait()
    little[1].wait()
    row_ref[...] = row_weights(z, here, ranks, scales)
    col_ref[...] = column_weights(z, here, ranks, scales)
    little[2].wait()
    for f in range(z.freqs):
        vectors = []
        for r in range(z.rows):
            at = slice(r * z.side, (r + 1) * z.side)
            vectors.append((recorded[f, 0, :, at], recorded[f, 1, :, at]))
        copies[f].wait()
        contract(z, left_block, u, f, vectors, 0, row_ref, out_ref)
    little[3].wait()
    little[4].wait()
    at = lax.broadcasted_iota(jnp.int32, scalars_ref.shape, 0)
    scalars = jnp.full(scalars_ref.shape, levels[lax.axis_index("freq") % z.team // (z.team // z.virtual)], F32)
    for f in range(z.freqs):
        scalars = jnp.where(at == f, steps[f], scalars)
    scalars_ref[...] = scalars


def source_rows(z, f, c, j, half):
    halves = z.side // 128
    start = (j * halves + half) * z.pairs + 2 * f + c
    return pl.ds(start, z.virtual, stride=padded(z))


def padded(z):
    return z.cols * (z.side // 128) * z.pairs + 8


def spread_rows(z, blocks, rows_ref):
    held = padded(z) - 8
    rows = blocks.astype(F32).reshape(z.virtual * held, 128)
    for v in range(z.virtual):
        rows_ref[v * padded(z) : v * padded(z) + held, :] = rows[v * held : (v + 1) * held]


def gather_rows(z, rows_ref):
    held = padded(z) - 8
    rows = [rows_ref[v * padded(z) : v * padded(z) + held, :] for v in range(z.virtual)]
    return jnp.concatenate(rows, 0).reshape(z.team, -1, 128)


def gradient(z, right, f, arrived_ref, scalars_ref, rows_ref):
    high = 2 * z.virtual
    total = combine(z, right_block, right, f, arrived_ref, 1, z.cols)
    for j in range(z.cols):
        for c in range(2):
            start = j * high + c * z.virtual
            for half in range(z.side // 128):
                part = total[start : start + z.virtual, half * 128 : (half + 1) * 128]
                rows_ref[source_rows(z, f, c, j, half), :] = part * scalars_ref[f : f + 1, :]


def encode(x):
    w = jnp.abs(x) * (1.0 / KNEE)
    t = w + jnp.sqrt(w * w + 1.0)
    square = t * t
    fifth = square * square * t * 2.0**-60
    return jnp.where(x < 0.0, -fifth * fifth, fifth * fifth).astype(BF16)


def decode(code):
    z = code.astype(F32)
    angle = (jnp.log(jnp.abs(z)) + 120.0 * math.log(2.0)) * 0.1
    size = (jnp.exp(angle) - jnp.exp(-angle)) * (0.5 * KNEE)
    return jnp.where(z < 0.0, -size, size)


def send_twice(z, blocks, out_ref):
    for team in range(2):
        out_ref[team * z.team : (team + 1) * z.team] = blocks


def first_gradient_kernel(z, right, arrived_ref, scalars_ref, out_ref, rows_ref):
    for f in range(z.freqs):
        gradient(z, right, f, arrived_ref, scalars_ref, rows_ref)
    send_twice(z, encode(gather_rows(z, rows_ref)), out_ref)


def second_gradient_kernel(z, right, arrived_ref, scalars_ref, out_ref, rows_ref):
    for f in range(z.freqs):
        gradient(z, right, f, arrived_ref, scalars_ref, rows_ref)
    send_twice(z, gather_rows(z, rows_ref).astype(BF16), out_ref)


def times(table, x):
    high = x.astype(BF16)
    low = (x - high.astype(F32)).astype(BF16)
    return jnp.dot(table, jnp.concatenate([high, low, high], 0), preferred_element_type=F32)


def threshold(z, field, tables_ref, scalars_ref):
    signal = times(tables_ref[0], field)
    level = jnp.concatenate([scalars_ref[z.freqs : z.freqs + 1, :]] * (field.shape[1] // 128), 1)
    return signal - jnp.clip(signal, -level, level)


def send_back(z, mine, out_ref):
    parts = [
        mine[:, lo : lo + 128].reshape(z.team, z.pairs, 128) for lo in range(0, mine.shape[1], 128)
    ]
    out_ref[...] = jnp.concatenate(parts, 1).astype(BF16)


def field_of(z, blocks):
    parts = [
        blocks[:, lo : lo + z.pairs].reshape(z.times, 128) for lo in range(0, blocks.shape[1], z.pairs)
    ]
    return jnp.concatenate(parts, 1)


def team_rows(z):
    count = z.team * z.pairs
    return pl.ds(pl.multiple_of(lax.axis_index("freq") // z.team * count, count), count)


def first_threshold_kernel(z, arrived_ref, tables_ref, scalars_ref, out_ref, first_ref):
    kept = threshold(z, field_of(z, decode(arrived_ref[...])), tables_ref, scalars_ref)
    first_ref[...] = times(tables_ref[1], kept).astype(first_ref.dtype)
    send_back(z, first_ref[team_rows(z), :], out_ref)


def second_threshold_kernel(z, arrived_ref, first_ref, tables_ref, scalars_ref, out_ref):
    field = first_ref[...] + field_of(z, arrived_ref[...].astype(F32))
    kept = threshold(z, field, tables_ref, scalars_ref)
    send_back(z, times(tables_ref[1, team_rows(z), :], kept), out_ref)


def field_rows(z, ref, f, c, j):
    return jnp.concatenate([ref[source_rows(z, f, c, j, half), :] for half in range(z.side // 128)], 1)


def coefficients_kernel(z, right, field_ref, weights_ref, out_ref, rows_ref):
    spread_rows(z, field_ref[...], rows_ref)
    for f in range(z.freqs):
        vectors = [(field_rows(z, rows_ref, f, 0, j), field_rows(z, rows_ref, f, 1, j)) for j in range(z.cols)]
        contract(z, right_block, right, f, vectors, 1, weights_ref, out_ref)


def residual_kernel(z, left, arrived_ref, recorded_ref, weights_ref, out_ref):
    v = z.virtual
    images = [combine(z, left_block, left, f, arrived_ref, 0, z.rows) for f in range(z.freqs)]
    for f, image in enumerate(images):
        vectors = []
        for r in range(z.rows):
            at = slice(r * z.side, (r + 1) * z.side)
            start = 2 * r * v
            vectors.append(
                (
                    recorded_ref[f, 0, :, at] - image[start : start + v],
                    recorded_ref[f, 1, :, at] - image[start + v : start + 2 * v],
                )
            )
        contract(z, left_block, left, f, vectors, 0, weights_ref, out_ref)


def output_kernel(z, field_ref, out_hbm, rows_ref, held, sems):
    spread_rows(z, field_ref[...], rows_ref)
    copies = []
    for f in range(z.freqs):
        for c in range(2):
            for j in range(z.cols):
                held[f, c, :, j * z.side : (j + 1) * z.side] = field_rows(z, rows_ref, f, c, j)
        copies.append(pltpu.make_async_copy(held.at[f], out_hbm.at[f], sems.at[f]))
        copies[f].start()
    for copy in copies:
        copy.wait()


def dft_tables(freqs, times):
    f = np.arange(freqs)[:, None]
    t = np.arange(times)[None, :]
    angles = ((f * t) % times) * (2.0 * math.pi / times)
    scaling = np.where(f == 0, math.sqrt(1.0 / times), math.sqrt(2.0 / times))
    both = np.stack([scaling * np.cos(angles), -scaling * np.sin(angles)], 1)
    forth = np.ascontiguousarray(both.reshape(2 * freqs, times).T.astype(np.float32))
    sides = []
    for table in (forth, forth.T):
        high = table.astype(ml_dtypes.bfloat16)
        low = (table - high.astype(np.float32)).astype(ml_dtypes.bfloat16)
        sides.append(np.concatenate([high, high, low], 1))
    return np.stack(sides)


HBM = pl.BlockSpec(memory_space=pltpu.HBM)
VMEM = pl.BlockSpec(memory_space=pltpu.VMEM)


def run(name, kernel, in_specs, out, scratch=(), out_specs=VMEM, cost=None):
    return pl.pallas_call(
        kernel,
        name=name,
        in_specs=in_specs,
        out_specs=out_specs if isinstance(out, jax.ShapeDtypeStruct) else [out_specs] * len(out),
        out_shape=out,
        scratch_shapes=list(scratch),
        interpret=INTERPRET,
        cost_estimate=cost,
        compiler_params=pltpu.CompilerParams(vmem_limit_bytes=40 << 20),
    )


def per_device(left, right, tile_ranks, tile_scales, recorded, step_sizes, thresholds, tiles, groups):
    z = Sizes(left, right, recorded, tiles, groups)
    part = functools.partial
    shape = jax.ShapeDtypeStruct
    halves = z.side // 128
    coefs = shape((z.tiles, z.freqs, 2 * z.virtual, z.lanes), BF16)
    weights = shape((z.freqs * z.tiles, z.lanes), F32)
    rows = (z.virtual * padded(z), 128)
    forth = shape((z.groups, 2 * halves * z.pairs, 128), BF16)
    back = shape((z.team, 2 * halves * z.pairs, 128), BF16)
    teams = [list(range(at, at + z.team)) for at in (0, z.team)]
    rows_scratch = [pltpu.VMEM(rows, F32)]
    tables = jnp.asarray(dft_tables(z.freqs * z.groups, z.times))

    def over_tile(x):
        return lax.all_to_all(x, "tile", split_axis=0, concat_axis=0, tiled=True)

    def over_freq(x):
        return lax.all_to_all(x, "freq", split_axis=0, concat_axis=0, tiled=True)

    def over_team(x):
        return lax.all_to_all(x, "freq", split_axis=0, concat_axis=0, tiled=True, axis_index_groups=teams)

    def far(x):
        return pltpu.with_memory_space_constraint(x, pltpu.HBM)

    held = [pltpu.VMEM(x.shape, x.dtype) for x in (left, recorded, tile_ranks, tile_scales)]
    held += [pltpu.SMEM(x.shape, x.dtype) for x in (step_sizes, thresholds)]
    held += [pltpu.SemaphoreType.DMA((z.freqs,)), pltpu.SemaphoreType.DMA((5,))]
    duals, row_weight, col_weight, scalars = run(
        "first_duals", part(first_duals_kernel, z), [HBM] * 6, [coefs, weights, weights, shape((8, 128), F32)], held
    )(far(left), far(recorded), far(tile_ranks), far(tile_scales), far(step_sizes), far(thresholds))
    update = run("first_gradient", part(first_gradient_kernel, z), [VMEM] * 3, forth, rows_scratch)(
        right, over_tile(duals), scalars
    )
    sent, first = run(
        "first_threshold", part(first_threshold_kernel, z), [VMEM] * 3, [back, shape((z.times, 2 * z.side), F32)]
    )(over_freq(update), tables, scalars)
    coeffs = run("coefficients", part(coefficients_kernel, z), [VMEM] * 3, coefs, rows_scratch)(
        right, over_team(sent), col_weight
    )
    duals = run("residual", part(residual_kernel, z), [VMEM] * 4, coefs)(
        left, over_tile(coeffs), recorded, row_weight
    )
    update = run("second_gradient", part(second_gradient_kernel, z), [VMEM] * 3, forth, rows_scratch)(
        right, over_tile(duals), scalars
    )
    sent = run("second_threshold", part(second_threshold_kernel, z), [VMEM] * 4, back)(
        over_freq(update), first, tables, scalars
    )
    out = shape((z.freqs, 2, z.virtual, z.cols * z.side), F32)
    held = rows_scratch + [pltpu.VMEM(out.shape, F32), pltpu.SemaphoreType.DMA((z.freqs,))]
    return run("output", part(output_kernel, z), [VMEM], out, held, HBM)(over_team(sent))


def solution(mesh):
    return jax.shard_map(
        functools.partial(per_device, tiles=mesh.shape["tile"], groups=mesh.shape["freq"]),
        mesh=mesh,
        in_specs=(
            P("freq", "tile", None, None, None, None),
            P("freq", None, "tile", None, None, None),
            P("freq", None, None),
            P("freq", None, None, None),
            P("freq", None, None, "tile"),
            P("freq"),
            P(),
        ),
        out_specs=P("freq", None, None, "tile"),
        check_vma=False,
    )
```
